128 devices in a mesh: tm: 8 (over z, y_hi), dof: 16 (over x, y_lo, core).
Axes of the slice: x: 4, y: 4 (y_hi: 2, y_lo: 2; y = y_hi * 2 + y_lo), z: 4, core: 2. Of those that a mesh axis runs over, the one named last changes fastest.
Arguments:
- loads: bfloat16 [3072, 8192], P('tm', 'dof'), may hold values from -6 to 6
- phi: bfloat16 [12288, 4096], P('dof'), may hold values from -0.09375 to 0.09375
- load_index: int32 [8192], P('dof'), may hold values from 0 to 12287, as said below
- damping: float32 [4096], P('dof'), may hold values from 6.510417e-05 to 0.05
- frequency: float32 [4096], P('dof'), may hold values from 0.05 to 1.5
- gains: float32 [3072], P('tm'), may hold values from 0.25 to 1
- shapes: bfloat16 [4096, 32768], P(None, 'dof'), may hold values from -0.09375 to 0.09375
Outputs:
- field: bfloat16 [3072, 32768], P('tm', 'dof')
- history: float32 [4096, 3072], P('dof', 'tm')
The draws below stay inside these ranges and needn't reach their ends.
Inputs may be any that keep to these rules, and one draw needn't show every extreme that they name: `load_index`: entries k * 512 to (k + 1) * 512 - 1 name rows k * 768 to (k + 1) * 768 - 1; rows may repeat.
All inputs are finite; a program needn't handle non-finite values.
Results may differ from the reference program's by a relative error of at most 0.0049.
Values may be sent and summed in bfloat16 or wider, within the bound.
No kernel may reach another device: no remote copies, remote signals or barrier semaphores. Data moves between devices by JAX's collectives and lax.ppermute only.
A program may use at most 128 MiB of HBM per device.

```python
import math
import jax
import jax.numpy as jnp
from jax import lax

M = 4096
LOAD_DEV = 512
DOF_DEV = 768
TIMES = 3072
LOADS = 8192
NDOF = 12288
NFP = 32768


def draw_load_index(key, part):
    places = jnp.arange(LOADS, dtype=jnp.int32)
    slot = places % LOAD_DEV
    local = jax.random.randint(key, (LOADS,), 0, DOF_DEV, dtype=jnp.int32)
    local = jnp.where(slot == 0, 0, jnp.where(slot == 1, DOF_DEV - 1, local))
    return places // LOAD_DEV * DOF_DEV + local


def draw_gains(key, part):
    first, second, third = jax.random.split(key, 3)
    spots = jax.random.randint(first, (4,), 0, TIMES, dtype=jnp.int32)
    depth = jax.random.uniform(second, (4,), jnp.float32, 0.2, 0.5)
    base = 1.0 - 0.0002 * jax.random.uniform(third, (TIMES,), jnp.float32)
    steps = jnp.arange(TIMES, dtype=jnp.int32)
    hit = steps[:, None] == spots[None, :]
    factor = jnp.prod(jnp.where(hit, 1.0 - depth[None, :], 1.0), axis=1)
    return (base * factor).astype(jnp.float32)


def with_spikes(values, own_key, source, target, parts, factor):
    def block_of(axis_at):
        return (jnp.arange(values.shape[axis_at]) // (values.shape[axis_at] // parts)).reshape((-1,) + (1,) * (values.ndim - 1 - axis_at))

    near = jax.random.permutation(own_key, parts)[block_of(target)]
    far = (block_of(target) + parts // 2) % parts
    return jnp.where((block_of(source) == near) | (block_of(source) == far), factor * values, values)


def block_levels(key, extent, cuts, low, high):
    loudness, own = 1.0, jax.random.fold_in(key, 6)
    for dim, shards_of in cuts:
        steps = jnp.exp(jax.random.uniform(jax.random.fold_in(own, dim), (shards_of,), jnp.float32, low / len(cuts), high / len(cuts)))
        loudness = loudness * jnp.repeat(steps, extent[dim] // shards_of).reshape([-1 if axis == dim else 1 for axis in range(len(extent))])
    return loudness


def normal_values(stream_key, dims, deviation, limit, cuts=(), held_as=jnp.bfloat16):
    values = jax.random.normal(stream_key, dims, jnp.float32) * deviation
    if len(cuts) > 0:
        values = block_levels(stream_key, dims, cuts, -0.22, 0.18) * values
    return jnp.clip(values, min=-limit, max=limit).astype(held_as)


def heavy_noise(stream_key, extent, deviation, bound, shards, heavy, kind=jnp.bfloat16):
    entries = deviation * jax.random.normal(stream_key, extent, jnp.float32)
    if shards:
        entries = entries * block_levels(stream_key, extent, shards, -0.22, 0.18)
    return jnp.clip(with_spikes(entries, jax.random.fold_in(stream_key, 3), *heavy), -bound, bound).astype(kind)


def setup_inputs(seed: int = 0) -> dict:
    key_of = jax.random.split(jax.random.key(seed), 8)
    return {
        "loads": normal_values(key_of[0], (TIMES, LOADS), 1.0, 6.0, ((0, 8), (1, 16))),
        "phi": heavy_noise(key_of[1], (NDOF, M), LOADS ** -0.5, 0.09375, ((0, 16),), (0, 1, 16, 2.0)),
        "load_index": draw_load_index(jax.random.fold_in(key_of[7], 71), 0),
        "damping": jnp.clip(jnp.exp(math.log(0.05) - 6.64379 * jax.random.uniform(key_of[3], (M,), jnp.float32) ** block_levels(key_of[3], (M,), ((0, 16),), -0.2, 0.2)), 6.510417006211355e-05, 0.05),
        "frequency": jnp.clip(0.05 + 1.45 * jax.random.uniform(key_of[4], (M,), jnp.float32) ** block_levels(key_of[4], (M,), ((0, 16),), -0.2, 0.2), 0.05, 1.5),
        "gains": draw_gains(jax.random.fold_in(key_of[7], 71), 0),
        "shapes": normal_values(key_of[6], (M, NFP), M ** -0.5, 0.09375, ((1, 16),)),
    }


def combine(earlier, later):
    ear, eai, ebr, ebi = earlier
    lar, lai, lbr, lbi = later
    return (lar * ear - lai * eai, lar * eai + lai * ear, lar * ebr - lai * ebi + lbr, lar * ebi + lai * ebr + lbi)

def reference(loads, phi, load_index, damping, frequency, gains, shapes):
    selected = jnp.take(phi, load_index, axis=0)
    modal = jnp.dot(selected.T, loads.T, preferred_element_type=jnp.float32)
    radius = jnp.exp(-damping)
    drive = jnp.sqrt(-jnp.expm1(-2.0 * damping))
    coef_re = gains[None, :] * (radius * jnp.cos(frequency))[:, None]
    coef_im = gains[None, :] * (radius * jnp.sin(frequency))[:, None]
    push_re = drive[:, None] * modal
    push_im = jnp.zeros_like(push_re)
    result = lax.associative_scan(combine, (coef_re, coef_im, push_re, push_im), axis=1)
    history = result[2]
    rounded = history.astype(jnp.bfloat16)
    field = jnp.dot(rounded.T, shapes, preferred_element_type=jnp.float32).astype(jnp.bfloat16)
    return (field, history)
```

```python
import jax
import jax.numpy as jnp
from jax import lax
from jax.experimental import pallas as pl
from jax.experimental.pallas import tpu as pltpu
from jax.sharding import Mesh, PartitionSpec as P

TM = ("z", "yh")
XY = ("x", "yl")
DOF = ("x", "yl", "core")
F32 = jnp.float32
BF16 = jnp.bfloat16
LIMIT = 48 * 1024 * 1024


def vmem():
    return pl.BlockSpec(memory_space=pltpu.VMEM)


def scatter_kernel(index_ref, loads_ref, hi_ref, lo_ref):
    rows = hi_ref.shape[1]
    channels = index_ref.shape[1]
    place = lax.broadcasted_iota(jnp.int32, (rows, channels), 0)
    onehot = jnp.where(place == index_ref[...], 1.0, 0.0).astype(BF16)
    summed = lax.dot_general(
        loads_ref[...], onehot, (((1,), (1,)), ((), ())), preferred_element_type=F32
    )
    high = summed.astype(BF16)
    hi_ref[...] = high
    lo_ref[...] = (summed - high.astype(F32)).astype(BF16)


def scatter_loads(index_row, loads, rows):
    steps = loads.shape[0]
    shape = jax.ShapeDtypeStruct((steps, rows), BF16)
    return pl.pallas_call(
        scatter_kernel,
        out_shape=(shape, shape),
        in_specs=[vmem(), vmem()],
        out_specs=(vmem(), vmem()),
        name="scatter_loads",
    )(index_row, loads)


def partial_kernel(which_ref, hi_ref, lo_ref, phi_ref, out_ref):
    block = phi_ref[...]
    total = jnp.dot(hi_ref[...], block, preferred_element_type=F32)
    total += jnp.dot(lo_ref[...], block, preferred_element_type=F32)
    out_ref[0] = total.astype(out_ref.dtype)


def partial_modal(which, high, low, phi, owned, dtype):
    steps, rows = high.shape
    count = phi.shape[1] // owned // 2
    return pl.pallas_call(
        partial_kernel,
        out_shape=jax.ShapeDtypeStruct((count, steps, owned), dtype),
        grid_spec=pltpu.PrefetchScalarGridSpec(
            num_scalar_prefetch=1,
            grid=(count,),
            in_specs=[
                pl.BlockSpec((steps, rows), lambda i, w: (0, 0)),
                pl.BlockSpec((steps, rows), lambda i, w: (0, 0)),
                pl.BlockSpec((rows, owned), lambda i, w: (0, 2 * i + w[0])),
            ],
            out_specs=pl.BlockSpec((1, steps, owned), lambda i, w: (i, 0, 0)),
        ),
        cost_estimate=pl.CostEstimate(
            flops=4 * steps * rows * owned * count,
            bytes_accessed=rows * owned * count * 2,
            transcendentals=0,
        ),
        name="partial_modal",
    )(which, high, low, phi)


def coef_kernel(gain_ref, rows_ref, cr_ref, ci_ref, qr_ref, qi_ref, pre_ref, whole_ref):
    inner = gain_ref.shape[0]
    lanes = rows_ref.shape[1]
    zr = rows_ref[0:1, :]
    zi = rows_ref[1:2, :]
    reps = lanes // gain_ref.shape[2]
    qr = jnp.ones((8, lanes), F32)
    qi = jnp.zeros((8, lanes), F32)
    product = jnp.ones((8, gain_ref.shape[2]), F32)
    for j in range(inner):
        gain = gain_ref[j]
        product = product * gain
        gain = jnp.concatenate([gain] * reps, axis=1)
        cr = gain * zr
        ci = gain * zi
        cr_ref[j] = cr
        ci_ref[j] = ci
        qr, qi = qr * cr - qi * ci, qr * ci + qi * cr
        qr_ref[j] = qr
        qi_ref[j] = qi
    pr = jnp.ones((1, lanes), F32)
    pi = jnp.zeros((1, lanes), F32)
    total = jnp.ones((1, gain_ref.shape[2]), F32)
    for b in range(8):
        pre_ref[0, b : b + 1, :] = pr
        pre_ref[1, b : b + 1, :] = pi
        br = qr[b : b + 1, :]
        bi = qi[b : b + 1, :]
        pr, pi = pr * br - pi * bi, pr * bi + pi * br
        total = total * product[b : b + 1, :]
    whole_ref[...] = jnp.broadcast_to(jnp.concatenate([pr, pi], axis=1), whole_ref.shape)


def coefficients(gain_blocks, rows):
    inner = gain_blocks.shape[0]
    lanes = rows.shape[1]
    full = jax.ShapeDtypeStruct((inner, 8, lanes), F32)
    return pl.pallas_call(
        coef_kernel,
        out_shape=(
            full,
            full,
            full,
            full,
            jax.ShapeDtypeStruct((2, 8, lanes), F32),
            jax.ShapeDtypeStruct((8, 2 * lanes), F32),
        ),
        in_specs=[vmem(), vmem()],
        out_specs=(vmem(),) * 6,
        name="coefficients",
    )(gain_blocks, rows)


def local_kernel(parts_ref, rows_ref, cr_ref, ci_ref, qr_ref, qi_ref, whole_ref,
                 w_ref, enter_ref, send_ref, push_ref):
    count, steps, lanes = parts_ref.shape
    inner = steps // 8
    drive = rows_ref[2:3, :]
    tile = 64
    for s in range(0, steps, tile):
        total = parts_ref[0, s : s + tile, :].astype(F32)
        for c in range(1, count):
            total += parts_ref[c, s : s + tile, :].astype(F32)
        total *= drive
        push_ref[0, s : s + tile, :] = total[:, : lanes // 2]
        push_ref[1, s : s + tile, :] = total[:, lanes // 2 :]
    wr = jnp.zeros((8, lanes), F32)
    wi = jnp.zeros((8, lanes), F32)
    for j in range(inner):
        push = jnp.concatenate(
            [push_ref[h, pl.ds(j, 8, stride=inner), :] for h in range(2)], axis=1
        )
        cr = cr_ref[j]
        ci = ci_ref[j]
        wr, wi = cr * wr - ci * wi + push, cr * wi + ci * wr
        w_ref[j] = wr
    qr = qr_ref[inner - 1]
    qi = qi_ref[inner - 1]
    sr = jnp.zeros((1, lanes), F32)
    si = jnp.zeros((1, lanes), F32)
    for b in range(8):
        enter_ref[0, b : b + 1, :] = sr
        enter_ref[1, b : b + 1, :] = si
        br = qr[b : b + 1, :]
        bi = qi[b : b + 1, :]
        sr, si = (
            br * sr - bi * si + wr[b : b + 1, :],
            br * si + bi * sr + wi[b : b + 1, :],
        )
    send_ref[...] = jnp.concatenate(
        [jnp.broadcast_to(jnp.concatenate([sr, si], axis=1), (8, 2 * lanes)), whole_ref[...]],
        axis=1,
    )


def local_recurrence(parts, rows, cr, ci, qr, qi, whole):
    count, steps, lanes = parts.shape
    inner = steps // 8
    return pl.pallas_call(
        local_kernel,
        out_shape=(
            jax.ShapeDtypeStruct((inner, 8, lanes), F32),
            jax.ShapeDtypeStruct((2, 8, lanes), F32),
            jax.ShapeDtypeStruct((8, 4 * lanes), F32),
        ),
        in_specs=[vmem()] * 7,
        out_specs=(vmem(),) * 3,
        scratch_shapes=[pltpu.VMEM((2, steps, lanes // 2), F32)],
        compiler_params=pltpu.CompilerParams(vmem_limit_bytes=LIMIT),
        name="local_recurrence",
    )(parts, rows, cr, ci, qr, qi, whole)


def history_kernel(mine_ref, got_ref, enter_ref, pre_ref, w_ref, qr_ref, qi_ref,
                   history_ref, rounded_ref, hist_ref):
    inner, _, lanes = w_ref.shape
    mine = mine_ref[0]
    sr = jnp.zeros((1, lanes), F32)
    si = jnp.zeros((1, lanes), F32)
    for k in range(7):
        row = got_ref[k : k + 1, :]
        br = row[:, 0:lanes]
        bi = row[:, lanes : 2 * lanes]
        ar = row[:, 2 * lanes : 3 * lanes]
        ai = row[:, 3 * lanes : 4 * lanes]
        nr = ar * sr - ai * si + br
        ni = ar * si + ai * sr + bi
        take = jnp.full((1, lanes), mine, jnp.int32) > k
        sr = jnp.where(take, nr, sr)
        si = jnp.where(take, ni, si)
    er = enter_ref[0] + pre_ref[0] * sr - pre_ref[1] * si
    ei = enter_ref[1] + pre_ref[0] * si + pre_ref[1] * sr
    for j in range(inner):
        value = w_ref[j] + qr_ref[j] * er - qi_ref[j] * ei
        for h in range(2):
            hist_ref[h, pl.ds(j, 8, stride=inner), :] = value[
                :, h * (lanes // 2) : (h + 1) * (lanes // 2)
            ]
    for h in range(2):
        half = hist_ref[h]
        rounded_ref[:, h * (lanes // 2) : (h + 1) * (lanes // 2)] = half.astype(BF16)
        history_ref[h * (lanes // 2) : (h + 1) * (lanes // 2), :] = half.T


def make_history(mine, got, enter, pre, w, qr, qi):
    inner, _, lanes = w.shape
    steps = inner * 8
    return pl.pallas_call(
        history_kernel,
        out_shape=(
            jax.ShapeDtypeStruct((lanes, steps), F32),
            jax.ShapeDtypeStruct((steps, lanes), BF16),
        ),
        in_specs=[pl.BlockSpec(memory_space=pltpu.SMEM)] + [vmem()] * 6,
        out_specs=(vmem(), vmem()),
        scratch_shapes=[pltpu.VMEM((2, steps, lanes // 2), F32)],
        name="make_history",
    )(mine, got, enter, pre, w, qr, qi)


def field_kernel(core_ref, near_ref, far_ref, even_ref, odd_ref, out_ref, acc_ref):
    step = pl.program_id(0)
    core = core_ref[0]

    @pl.when(step == 0)
    def _():
        acc_ref[...] = jnp.zeros_like(acc_ref)

    total = jnp.dot(near_ref[0], even_ref[0, 0], preferred_element_type=F32)
    total += jnp.dot(far_ref[0], odd_ref[0, 0], preferred_element_type=F32)
    acc_ref[...] += total

    @pl.when(step == pl.num_programs(0) - 1)
    def _():
        out_ref[...] = acc_ref[...].astype(BF16)


def make_field(core, near, far, shapes):
    count, steps, lanes = near.shape
    points = shapes.shape[1]
    view = shapes.reshape(count, 2, lanes, points)
    return pl.pallas_call(
        field_kernel,
        out_shape=jax.ShapeDtypeStruct((steps, points), BF16),
        grid_spec=pltpu.PrefetchScalarGridSpec(
            num_scalar_prefetch=1,
            grid=(count,),
            in_specs=[
                pl.BlockSpec((1, steps, lanes), lambda i, c: (i, 0, 0)),
                pl.BlockSpec((1, steps, lanes), lambda i, c: (i, 0, 0)),
                pl.BlockSpec((1, 1, lanes, points), lambda i, c: (i, c[0], 0, 0)),
                pl.BlockSpec((1, 1, lanes, points), lambda i, c: (i, 1 - c[0], 0, 0)),
            ],
            out_specs=pl.BlockSpec((steps, points), lambda i, c: (0, 0)),
            scratch_shapes=[pltpu.VMEM((steps, points), F32)],
        ),
        compiler_params=pltpu.CompilerParams(vmem_limit_bytes=LIMIT),
        name="make_field",
    )(core, near, far, view, view)


def body(loads, phi, load_index, damping, frequency, gains, shapes):
    owned = damping.shape[0]
    steps = loads.shape[0]
    rows_here = phi.shape[0]
    inner = steps // 8
    core = lax.axis_index("core").astype(jnp.int32).reshape(1)
    pair = [(0, 1), (1, 0)]
    index_row = (load_index - lax.axis_index(DOF) * rows_here).reshape(1, -1)

    high, low = scatter_loads(index_row, loads, rows_here)
    send = partial_modal(1 - core, high, low, phi, owned, BF16)
    got = lax.ppermute(send, "core", pair)
    keep = partial_modal(core, high, low, phi, owned, F32)

    radius = jnp.exp(-damping)
    drive = jnp.sqrt(-jnp.expm1(-2.0 * damping))
    nothing = jnp.zeros_like(drive)
    rows = jnp.stack(
        [radius * jnp.cos(frequency), radius * jnp.sin(frequency), drive] + [nothing] * 5
    )
    gain_blocks = jnp.broadcast_to(gains.reshape(8, inner).T[:, :, None], (inner, 8, 128))
    cr, ci, qr, qi, pre, whole = coefficients(gain_blocks, rows)

    summed = (keep + got.astype(F32)).astype(BF16)
    parts = lax.all_to_all(summed, XY, 0, 0)
    w, enter, payload = local_recurrence(parts, rows, cr, ci, qr, qi, whole)
    states = lax.all_to_all(payload, TM, 0, 0)
    mine = lax.axis_index(TM).astype(jnp.int32).reshape(1)
    history, rounded = make_history(mine, states, enter, pre, w, qr, qi)
    near = lax.all_to_all(jnp.broadcast_to(rounded[None], (8,) + rounded.shape), XY, 0, 0)
    far = lax.ppermute(near, "core", pair)
    field = make_field(core, near, far, shapes)
    return field, history


def solution(mesh):
    grid = Mesh(mesh.devices.reshape(4, 2, 4, 2, 2), ("z", "yh", "x", "yl", "core"))
    placed = (
        P(TM, DOF),
        P(DOF, None),
        P(DOF),
        P(DOF),
        P(DOF),
        P(TM),
        P(None, DOF),
    )
    return jax.shard_map(
        body,
        mesh=grid,
        in_specs=placed,
        out_specs=(P(TM, DOF), P(DOF, TM)),
        check_vma=False,
    )
```

```python
import jax
import jax.numpy as jnp
from jax import lax
from jax.experimental import pallas as pl
from jax.experimental.pallas import tpu as pltpu
from jax.sharding import Mesh, PartitionSpec as P

TM = ("z", "yh")
XY = ("x", "yl")
DOF = ("x", "yl", "core")
F32 = jnp.float32
BF16 = jnp.bfloat16
LANES = 256
HALF = 128
MID = 24 * 1024 * 1024
BIG = 40 * 1024 * 1024
STEPS = ((1, 0), (3, 0), (2, 0), (0, 1), (1, 1), (3, 1), (2, 1), (0, 0))
FIRST, LAST = (0, 1, 2, 3), (4, 5, 6, 7)


def vmem():
    return pl.BlockSpec(memory_space=pltpu.VMEM)


def cost(flops, moved):
    return pl.CostEstimate(flops=int(flops), bytes_accessed=int(moved), transcendentals=0)


def fetch_columns(columns_ref, phi_ref, held_ref, sems, chosen):
    copies = []
    for slot, q in enumerate(chosen):
        place = pl.multiple_of(columns_ref[q] * LANES, LANES)
        copies.append(
            pltpu.make_async_copy(
                phi_ref.at[:, pl.ds(place, LANES)], held_ref.at[slot], sems.at[slot]
            )
        )
    for copy in copies:
        copy.start()
    return copies


def open_kernel(chosen, columns_ref, index_ref, loads_ref, phi_ref, scat_ref, *refs):
    outs, held_ref, sems = refs[:-2], refs[-2], refs[-1]
    copies = fetch_columns(columns_ref, phi_ref, held_ref, sems, chosen)
    rows = scat_ref.shape[1]
    channels = index_ref.shape[1]
    local = index_ref[...] - lax.axis_index(DOF) * rows
    place = lax.broadcasted_iota(jnp.int32, (rows, channels), 0)
    onehot = jnp.where(place == local, 1.0, 0.0).astype(BF16)
    summed = lax.dot_general(
        loads_ref[...], onehot, (((1,), (1,)), ((), ())), preferred_element_type=F32
    )
    scat_ref[...] = summed.astype(BF16)
    for base in range(0, len(copies), 4):
        for copy in copies[base : base + 4]:
            copy.wait()
        block = jnp.concatenate([held_ref[base + q] for q in range(4)], axis=1)
        total = jnp.dot(scat_ref[...], block, preferred_element_type=F32)
        for q in range(4):
            outs[base + q][...] = total[:, q * LANES : (q + 1) * LANES].astype(BF16)


def more_kernel(chosen, mates, columns_ref, scat_ref, phi_ref, *refs):
    got, outs, held_ref, sems = refs[:mates], refs[mates:-2], refs[-2], refs[-1]
    copies = fetch_columns(columns_ref, phi_ref, held_ref, sems, chosen)
    for copy in copies:
        copy.wait()
    block = jnp.concatenate([held_ref[q] for q in range(len(copies))], axis=1)
    total = jnp.dot(scat_ref[...], block, preferred_element_type=F32)
    for q in range(len(copies)):
        value = total[:, q * LANES : (q + 1) * LANES] + got[q][...].astype(F32)
        outs[q][...] = value.astype(BF16)


def smem():
    return pl.BlockSpec(memory_space=pltpu.SMEM)


def hbm():
    return pl.BlockSpec(memory_space=pltpu.HBM)


def open_partial(columns, index_row, loads, phi, chosen):
    steps, channels = loads.shape
    rows = phi.shape[0]
    count = len(chosen)
    return pl.pallas_call(
        lambda *refs: open_kernel(chosen, *refs),
        out_shape=(jax.ShapeDtypeStruct((steps, rows), BF16),)
        + (jax.ShapeDtypeStruct((steps, LANES), BF16),) * count,
        in_specs=[smem(), vmem(), vmem(), hbm()],
        out_specs=(vmem(),) * (count + 1),
        scratch_shapes=[
            pltpu.VMEM((count, rows, LANES), BF16),
            pltpu.SemaphoreType.DMA((count,)),
        ],
        cost_estimate=cost(
            2 * steps * rows * (channels + count * LANES), 2 * rows * count * LANES
        ),
        compiler_params=pltpu.CompilerParams(vmem_limit_bytes=MID),
        name="open_partial",
    )(columns, index_row, loads, phi)


def more_partial(columns, scat, phi, chosen, got):
    steps, rows = scat.shape
    count = len(chosen)
    return pl.pallas_call(
        lambda *refs: more_kernel(chosen, len(got), *refs),
        out_shape=(jax.ShapeDtypeStruct((steps, LANES), BF16),) * count,
        in_specs=[smem(), vmem(), hbm()] + [vmem()] * len(got),
        out_specs=(vmem(),) * count,
        scratch_shapes=[
            pltpu.VMEM((count, rows, LANES), BF16),
            pltpu.SemaphoreType.DMA((count,)),
        ],
        cost_estimate=cost(2 * steps * rows * count * LANES, 2 * rows * count * LANES),
        compiler_params=pltpu.CompilerParams(vmem_limit_bytes=MID),
        name="more_partial",
    )(columns, scat, phi, *got)


def coef_kernel(gain_ref, rows_ref, cr_ref, ci_ref, qr_ref, qi_ref, pre_ref, whole_ref):
    inner = gain_ref.shape[0]
    zr = rows_ref[0:1, :]
    zi = rows_ref[1:2, :]
    qr = jnp.ones((8, LANES), F32)
    qi = jnp.zeros((8, LANES), F32)
    for j in range(inner):
        gain = jnp.concatenate([gain_ref[j]] * 2, axis=1)
        cr = gain * zr
        ci = gain * zi
        cr_ref[j] = cr
        ci_ref[j] = ci
        qr, qi = qr * cr - qi * ci, qr * ci + qi * cr
        qr_ref[j] = qr
        qi_ref[j] = qi
    pr = jnp.ones((1, LANES), F32)
    pi = jnp.zeros((1, LANES), F32)
    for b in range(8):
        pre_ref[0, b : b + 1, :] = pr
        pre_ref[1, b : b + 1, :] = pi
        br = qr[b : b + 1, :]
        bi = qi[b : b + 1, :]
        pr, pi = pr * br - pi * bi, pr * bi + pi * br
    whole_ref[0:1, :] = pr
    whole_ref[1:2, :] = pi
    whole_ref[2:3, :] = rows_ref[2:3, :]
    whole_ref[3:8, :] = jnp.zeros((5, LANES), F32)


def coefficients(gain_blocks, rows):
    inner = gain_blocks.shape[0]
    full = jax.ShapeDtypeStruct((inner, 8, LANES), F32)
    return pl.pallas_call(
        coef_kernel,
        out_shape=(
            full,
            full,
            full,
            full,
            jax.ShapeDtypeStruct((2, 8, LANES), F32),
            jax.ShapeDtypeStruct((8, LANES), F32),
        ),
        in_specs=[vmem(), vmem()],
        out_specs=(vmem(),) * 6,
        cost_estimate=cost(inner * 8 * LANES * 8, inner * 8 * LANES * 20),
        name="coefficients",
    )(gain_blocks, rows)


def local_kernel(*refs):
    parts = refs[:-9]
    cr_ref, ci_ref, qr_ref, qi_ref, whole_ref, w_ref, enter_ref, send_ref, push_ref = refs[-9:]
    steps = parts[0].shape[0]
    inner = steps // 8
    drive = whole_ref[2:3, :]
    tile = 64
    for s in range(0, steps, tile):
        total = parts[0][s : s + tile, :].astype(F32)
        for part in parts[1:]:
            total += part[s : s + tile, :].astype(F32)
        total = total * drive
        for h in range(2):
            push_ref[h, s : s + tile, :] = total[:, h * HALF : (h + 1) * HALF]
    wr = jnp.zeros((8, LANES), F32)
    wi = jnp.zeros((8, LANES), F32)
    for j in range(inner):
        push = jnp.concatenate(
            [push_ref[h, pl.ds(j, 8, stride=inner), :] for h in range(2)], axis=1
        )
        cr = cr_ref[j]
        ci = ci_ref[j]
        wr, wi = cr * wr - ci * wi + push, cr * wi + ci * wr
        w_ref[j] = wr
    qr = qr_ref[inner - 1]
    qi = qi_ref[inner - 1]
    sr = jnp.zeros((1, LANES), F32)
    si = jnp.zeros((1, LANES), F32)
    for b in range(8):
        enter_ref[0, b : b + 1, :] = sr
        enter_ref[1, b : b + 1, :] = si
        br = qr[b : b + 1, :]
        bi = qi[b : b + 1, :]
        sr, si = (
            br * sr - bi * si + wr[b : b + 1, :],
            br * si + bi * sr + wi[b : b + 1, :],
        )
    row = lax.broadcasted_iota(jnp.int32, (8, LANES), 0)
    tile = jnp.where(row == 0, sr, jnp.where(row == 1, si, 0.0))
    tile = jnp.where(row == 2, whole_ref[0:1, :], jnp.where(row == 3, whole_ref[1:2, :], tile))
    for k in range(send_ref.shape[0]):
        send_ref[k] = tile


def local_recurrence(parts, cr, ci, qr, qi, whole, groups):
    count, steps = len(parts), parts[0].shape[0]
    inner = steps // 8
    return pl.pallas_call(
        local_kernel,
        out_shape=(
            jax.ShapeDtypeStruct((inner, 8, LANES), F32),
            jax.ShapeDtypeStruct((2, 8, LANES), F32),
            jax.ShapeDtypeStruct((groups, 8, LANES), F32),
        ),
        in_specs=[vmem()] * (count + 5),
        out_specs=(vmem(),) * 3,
        scratch_shapes=[pltpu.VMEM((2, steps, HALF), F32)],
        cost_estimate=cost(steps * LANES * 16, steps * LANES * (2 * count + 12)),
        name="local_recurrence",
    )(*parts, cr, ci, qr, qi, whole)


def history_kernel(got_ref, enter_ref, pre_ref, w_ref, qr_ref, qi_ref, history_ref, out_ref, hist_ref):
    inner = w_ref.shape[0]
    mine = lax.axis_index(TM)
    sr = jnp.zeros((1, LANES), F32)
    si = jnp.zeros((1, LANES), F32)
    for k in range(got_ref.shape[0] - 1):
        tile = got_ref[k]
        br, bi, ar, ai = (tile[r : r + 1, :] for r in range(4))
        nr = ar * sr - ai * si + br
        ni = ar * si + ai * sr + bi
        take = mine > k
        sr = jnp.where(take, nr, sr)
        si = jnp.where(take, ni, si)
    er = enter_ref[0] + pre_ref[0] * sr - pre_ref[1] * si
    ei = enter_ref[1] + pre_ref[0] * si + pre_ref[1] * sr
    for j in range(inner):
        value = w_ref[j] + qr_ref[j] * er - qi_ref[j] * ei
        for h in range(2):
            hist_ref[h, pl.ds(j, 8, stride=inner), :] = value[:, h * HALF : (h + 1) * HALF]
    natural = jnp.concatenate([hist_ref[h] for h in range(2)], axis=1)
    history_ref[...] = natural
    rounded = natural.astype(BF16)
    for k in range(out_ref.shape[0]):
        out_ref[k] = rounded


def make_history(got, enter, pre, w, qr, qi, copies):
    inner = w.shape[0]
    steps = inner * 8
    return pl.pallas_call(
        history_kernel,
        out_shape=(
            jax.ShapeDtypeStruct((steps, LANES), F32),
            jax.ShapeDtypeStruct((copies, steps, LANES), BF16),
        ),
        in_specs=[vmem()] * 6,
        out_specs=(vmem(), vmem()),
        scratch_shapes=[pltpu.VMEM((2, steps, HALF), F32)],
        cost_estimate=cost(steps * LANES * 4, steps * LANES * 18),
        name="make_history",
    )(got, enter, pre, w, qr, qi)


def turn_kernel(natural_ref, out_ref):
    for h in range(2):
        part = slice(h * HALF, (h + 1) * HALF)
        out_ref[part, :] = natural_ref[:, part].T


def turn_history(natural):
    steps, lanes = natural.shape
    return pl.pallas_call(
        turn_kernel,
        out_shape=jax.ShapeDtypeStruct((lanes, steps), F32),
        in_specs=[vmem()],
        out_specs=vmem(),
        cost_estimate=cost(steps * lanes, steps * lanes * 8),
        name="turn_history",
    )(natural)


def field_kernel(which_ref, held_ref, shapes_ref, *refs):
    out_ref = refs[-1]
    total = None
    for i in range(held_ref.shape[0]):
        part = jnp.dot(held_ref[i], shapes_ref[i, 0], preferred_element_type=F32)
        total = part if total is None else total + part
    if len(refs) == 2:
        total = total + refs[0][...]
    out_ref[...] = total.astype(out_ref.dtype)


def add_field(which, held, shapes, before=None):
    count, steps, _ = held.shape
    points = shapes.shape[1]
    wide = 512
    view = shapes.reshape(count, 2, LANES, points)
    result = pl.BlockSpec((steps, wide), lambda n, c: (0, n))
    extra = [] if before is None else [before]
    return pl.pallas_call(
        field_kernel,
        out_shape=jax.ShapeDtypeStruct((steps, points), F32 if before is None else BF16),
        grid_spec=pltpu.PrefetchScalarGridSpec(
            num_scalar_prefetch=1,
            grid=(points // wide,),
            in_specs=[
                pl.BlockSpec((count, steps, LANES), lambda n, c: (0, 0, 0)),
                pl.BlockSpec((count, 1, LANES, wide), lambda n, c: (0, c[0], 0, n)),
            ]
            + [result] * len(extra),
            out_specs=result,
        ),
        compiler_params=pltpu.CompilerParams(vmem_limit_bytes=BIG),
        cost_estimate=cost(2 * count * LANES * steps * points, 2 * count * LANES * points),
        name="add_field",
    )(which, held, view, *extra)


def step_pairs(dx, dy):
    nx, ny = 4, 2
    return [
        (x * ny + y, (x + dx) % nx * ny + (y + dy) % ny) for x in range(nx) for y in range(ny)
    ]


def body(loads, phi, load_index, damping, frequency, gains, shapes):
    steps = loads.shape[0]
    inner = steps // 8
    groups = lax.axis_size(TM)
    core = lax.axis_index("core").astype(jnp.int32)
    x = lax.axis_index("x").astype(jnp.int32)
    y = lax.axis_index("yl").astype(jnp.int32)
    pair = [(0, 1), (1, 0)]
    ahead = jnp.stack([((x + dx) % 4) * 2 + (y + dy) % 2 for dx, dy in STEPS])

    theirs, ours = 2 * ahead + 1 - core, 2 * ahead + core
    phi = pltpu.with_memory_space_constraint(phi, pltpu.HBM)
    scat, *sent = open_partial(theirs, load_index.reshape(1, -1), loads, phi, FIRST + LAST)
    mates = [lax.ppermute(part, "core", pair) for part in sent]
    first, last = mates[:4], mates[4:]
    parts = []
    for chosen, mates in ((FIRST, first), (LAST, last)):
        summed = more_partial(ours, scat, phi, chosen, mates)
        for q, part in zip(chosen, summed):
            here = STEPS[q] == (0, 0)
            parts.append(part if here else lax.ppermute(part, XY, step_pairs(*STEPS[q])))

    radius = jnp.exp(-damping)
    drive = jnp.sqrt(-jnp.expm1(-2.0 * damping))
    nothing = jnp.zeros_like(drive)
    rows = jnp.stack(
        [radius * jnp.cos(frequency), radius * jnp.sin(frequency), drive] + [nothing] * 5
    )
    gain_blocks = jnp.broadcast_to(gains.reshape(8, inner).T[:, :, None], (inner, 8, HALF))

    cr, ci, qr, qi, pre, whole = coefficients(gain_blocks, rows)
    w, enter, payload = local_recurrence(parts, cr, ci, qr, qi, whole, groups)
    states = lax.all_to_all(payload, TM, 0, 0)
    natural, out = make_history(states, enter, pre, w, qr, qi, lax.axis_size(XY))
    near = lax.all_to_all(out, XY, 0, 0)
    history = turn_history(natural)
    far = lax.ppermute(near, "core", pair)
    which = core.reshape(1)
    field = add_field(which, near, shapes)
    field = add_field(1 - which, far, shapes, field)
    return field, history


def solution(mesh):
    grid = Mesh(mesh.devices.reshape(4, 2, 4, 2, 2), ("z", "yh", "x", "yl", "core"))
    placed = (
        P(TM, DOF),
        P(DOF, None),
        P(DOF),
        P(DOF),
        P(DOF),
        P(TM),
        P(None, DOF),
    )
    return jax.shard_map(
        body,
        mesh=grid,
        in_specs=placed,
        out_specs=(P(TM, DOF), P(DOF, TM)),
        check_vma=False,
    )
```

```python
import jax
import jax.numpy as jnp
from jax import lax
from jax.experimental import pallas as pl
from jax.experimental.pallas import tpu as pltpu
from jax.sharding import Mesh, PartitionSpec as P

TM = ("z", "yh")
XY = ("x", "yl")
DOF = ("x", "yl", "core")
F32 = jnp.float32
BF16 = jnp.bfloat16
LANES = 256
HALF = 128
MID = 12 * 1024 * 1024
STEPS = ((1, 0), (3, 0), (2, 0), (0, 1), (1, 1), (3, 1), (2, 1), (0, 0))


def vmem():
    return pl.BlockSpec(memory_space=pltpu.VMEM)


def cost(flops, moved):
    return pl.CostEstimate(flops=int(flops), bytes_accessed=int(moved), transcendentals=0)


def smem():
    return pl.BlockSpec(memory_space=pltpu.SMEM)


def hbm():
    return pl.BlockSpec(memory_space=pltpu.HBM)


def in_hbm(value):
    return pltpu.with_memory_space_constraint(value, pltpu.HBM)


def block_of(step, other):
    dx, dy = step
    x = lax.rem(lax.axis_index("x") + dx, 4)
    y = lax.rem(lax.axis_index("yl") + dy, 2)
    core = lax.axis_index("core")
    core = 1 - core if other else core
    return pl.multiple_of((2 * (2 * x + y) + core) * LANES, LANES)


def column_copies(steps, other, phi_ref, held_ref, sems):
    copies = []
    for q, step in enumerate(steps):
        columns = pl.ds(block_of(step, other), LANES)
        copies.append(
            pltpu.make_async_copy(phi_ref.at[:, columns], held_ref.at[q], sems.at[q])
        )
    return copies


def four_products(scat, held_ref, first):
    block = jnp.concatenate([held_ref[first + q] for q in range(4)], axis=1)
    total = jnp.dot(scat, block, preferred_element_type=F32)
    return [total[:, q * LANES : (q + 1) * LANES] for q in range(4)]


def open_kernel(index_hbm, loads_hbm, phi_ref, scat_ref, sent_ref, later_ref, kept_ref,
                index_ref, loads_ref, held_ref, sems, later_sems, kept_sems, load_sems):
    index_copy = pltpu.make_async_copy(index_hbm, index_ref, load_sems.at[0])
    loads_copy = pltpu.make_async_copy(loads_hbm, loads_ref, load_sems.at[1])
    copies = column_copies(STEPS[:4], True, phi_ref, held_ref, sems)
    after = column_copies(STEPS[4:], True, phi_ref, later_ref, later_sems)
    after += column_copies(STEPS, False, phi_ref, kept_ref, kept_sems)
    for copy in [index_copy, loads_copy] + copies + after:
        copy.start()
    rows = scat_ref.shape[1]
    channels = index_ref.shape[1]
    place = lax.broadcasted_iota(jnp.int32, (rows, channels), 0)
    index_copy.wait()
    local = index_ref[...] - lax.axis_index(DOF) * rows
    onehot = jnp.where(place == local, 1.0, 0.0).astype(BF16)
    loads_copy.wait()
    summed = lax.dot_general(
        loads_ref[...], onehot, (((1,), (1,)), ((), ())), preferred_element_type=F32
    )
    scat_ref[...] = summed.astype(BF16)
    for copy in copies:
        copy.wait()
    for q, value in enumerate(four_products(scat_ref[...], held_ref, 0)):
        sent_ref[q] = value.astype(BF16)
    for copy in after:
        copy.wait()


def open_partial(index_row, loads, phi):
    steps, channels = loads.shape
    rows = phi.shape[0]
    return pl.pallas_call(
        open_kernel,
        out_shape=(
            pltpu.VMEM((steps, rows), BF16),
            jax.ShapeDtypeStruct((4, steps, LANES), BF16),
            pltpu.VMEM((4, rows, LANES), BF16),
            pltpu.VMEM((8, rows, LANES), BF16),
        ),
        in_specs=[hbm(), hbm(), hbm()],
        out_specs=(vmem(),) * 4,
        scratch_shapes=[
            pltpu.VMEM((1, channels), jnp.int32),
            pltpu.VMEM((steps, channels), BF16),
            pltpu.VMEM((4, rows, LANES), BF16),
            pltpu.SemaphoreType.DMA((4,)),
            pltpu.SemaphoreType.DMA((4,)),
            pltpu.SemaphoreType.DMA((8,)),
            pltpu.SemaphoreType.DMA((2,)),
        ],
        cost_estimate=cost(2 * steps * rows * (channels + 4 * LANES), 32 * rows * LANES),
        compiler_params=pltpu.CompilerParams(vmem_limit_bytes=MID),
        name="open_partial",
    )(in_hbm(index_row), in_hbm(loads), in_hbm(phi))


def rest_kernel(scat_ref, later_ref, sent_ref):
    for q, value in enumerate(four_products(scat_ref[...], later_ref, 0)):
        sent_ref[q] = value.astype(BF16)


def rest_partial(scat, later):
    steps, rows = scat.shape
    return pl.pallas_call(
        rest_kernel,
        out_shape=jax.ShapeDtypeStruct((4, steps, LANES), BF16),
        in_specs=[vmem(), vmem()],
        out_specs=vmem(),
        cost_estimate=cost(8 * steps * rows * LANES, 8 * rows * LANES),
        compiler_params=pltpu.CompilerParams(vmem_limit_bytes=MID),
        name="rest_partial",
    )(scat, later)


def more_kernel(first, scat_ref, kept_ref, got_ref, *outs):
    for q, value in enumerate(four_products(scat_ref[...], kept_ref, first)):
        outs[q][...] = (value + got_ref[q].astype(F32)).astype(BF16)


def more_partial(scat, kept, first, got):
    steps, rows = scat.shape
    return pl.pallas_call(
        lambda *refs: more_kernel(first, *refs),
        out_shape=(jax.ShapeDtypeStruct((steps, LANES), BF16),) * 4,
        in_specs=[vmem()] * 3,
        out_specs=(vmem(),) * 4,
        cost_estimate=cost(8 * steps * rows * LANES, 8 * rows * LANES),
        compiler_params=pltpu.CompilerParams(vmem_limit_bytes=MID),
        name="more_partial",
    )(scat, kept, got)


def coef_kernel(gains_ref, zr_ref, zi_ref, drive_ref, shapes_ref,
                cr_ref, ci_ref, qr_ref, qi_ref, pre_ref, whole_ref, staged_ref, sems):
    tall = staged_ref.shape[0] // 8
    copies = []
    for q in range(8):
        part = pl.ds(q * tall, tall)
        copies.append(pltpu.make_async_copy(shapes_ref.at[part], staged_ref.at[part], sems.at[q]))
    for copy in copies:
        copy.start()
    steps = gains_ref.shape[1]
    inner = steps // 8
    row = lax.broadcasted_iota(jnp.int32, (steps, steps), 0)
    wanted = lax.rem(row, 8) * inner + lax.div(row, 8)
    hit = lax.broadcasted_iota(jnp.int32, (steps, steps), 1) == wanted
    left = gains_ref[...]
    gain_all = jnp.zeros((steps, LANES), F32)
    ones = jnp.ones((steps, LANES), BF16)
    for _ in range(3):
        term = left.astype(BF16)
        left = left - term.astype(F32)
        chosen = jnp.where(hit, term.astype(F32), 0.0).astype(BF16)
        gain_all = gain_all + jnp.dot(chosen, ones, preferred_element_type=F32)
    zr = zr_ref[...]
    zi = zi_ref[...]
    qr = jnp.ones((8, LANES), F32)
    qi = jnp.zeros((8, LANES), F32)
    for j in range(inner):
        gain = gain_all[8 * j : 8 * j + 8, :]
        cr = gain * zr
        ci = gain * zi
        cr_ref[j] = cr
        ci_ref[j] = ci
        qr, qi = qr * cr - qi * ci, qr * ci + qi * cr
        qr_ref[j] = qr
        qi_ref[j] = qi
    pr = jnp.ones((1, LANES), F32)
    pi = jnp.zeros((1, LANES), F32)
    for b in range(8):
        pre_ref[0, b : b + 1, :] = pr
        pre_ref[1, b : b + 1, :] = pi
        br = qr[b : b + 1, :]
        bi = qi[b : b + 1, :]
        pr, pi = pr * br - pi * bi, pr * bi + pi * br
    whole_ref[0:1, :] = pr
    whole_ref[1:2, :] = pi
    whole_ref[2:3, :] = drive_ref[...]
    whole_ref[3:8, :] = jnp.zeros((5, LANES), F32)
    for copy in copies:
        copy.wait()


def coefficients(gains, zr, zi, drive, shapes):
    inner = gains.shape[1] // 8
    full = jax.ShapeDtypeStruct((inner, 8, LANES), F32)
    return pl.pallas_call(
        coef_kernel,
        out_shape=(
            full,
            full,
            full,
            full,
            jax.ShapeDtypeStruct((2, 8, LANES), F32),
            jax.ShapeDtypeStruct((8, LANES), F32),
            pltpu.VMEM(shapes.shape, shapes.dtype),
        ),
        in_specs=[vmem()] * 4 + [hbm()],
        out_specs=(vmem(),) * 7,
        scratch_shapes=[pltpu.SemaphoreType.DMA((8,))],
        cost_estimate=cost(inner * 64 * LANES, 2 * shapes.size),
        compiler_params=pltpu.CompilerParams(vmem_limit_bytes=MID),
        name="coefficients",
    )(gains, zr, zi, drive, in_hbm(shapes))


def local_kernel(*refs):
    parts = refs[:-9]
    cr_ref, ci_ref, qr_ref, qi_ref, whole_ref, w_ref, enter_ref, send_ref, push_ref = refs[-9:]
    steps = parts[0].shape[0]
    inner = steps // 8
    drive = whole_ref[2:3, :]
    tile = 64
    for s in range(0, steps, tile):
        total = parts[0][s : s + tile, :].astype(F32)
        for part in parts[1:]:
            total += part[s : s + tile, :].astype(F32)
        total = total * drive
        for h in range(2):
            push_ref[h, s : s + tile, :] = total[:, h * HALF : (h + 1) * HALF]
    wr = jnp.zeros((8, LANES), F32)
    wi = jnp.zeros((8, LANES), F32)
    for j in range(inner):
        push = jnp.concatenate(
            [push_ref[h, pl.ds(j, 8, stride=inner), :] for h in range(2)], axis=1
        )
        cr = cr_ref[j]
        ci = ci_ref[j]
        wr, wi = cr * wr - ci * wi + push, cr * wi + ci * wr
        w_ref[j] = wr
    qr = qr_ref[inner - 1]
    qi = qi_ref[inner - 1]
    sr = jnp.zeros((1, LANES), F32)
    si = jnp.zeros((1, LANES), F32)
    for b in range(8):
        enter_ref[0, b : b + 1, :] = sr
        enter_ref[1, b : b + 1, :] = si
        br = qr[b : b + 1, :]
        bi = qi[b : b + 1, :]
        sr, si = (
            br * sr - bi * si + wr[b : b + 1, :],
            br * si + bi * sr + wi[b : b + 1, :],
        )
    row = lax.broadcasted_iota(jnp.int32, (8, LANES), 0)
    tile = jnp.where(row == 0, sr, jnp.where(row == 1, si, 0.0))
    tile = jnp.where(row == 2, whole_ref[0:1, :], jnp.where(row == 3, whole_ref[1:2, :], tile))
    for k in range(send_ref.shape[0]):
        send_ref[k] = tile


def local_recurrence(parts, cr, ci, qr, qi, whole, groups):
    count, steps = len(parts), parts[0].shape[0]
    inner = steps // 8
    return pl.pallas_call(
        local_kernel,
        out_shape=(
            jax.ShapeDtypeStruct((inner, 8, LANES), F32),
            jax.ShapeDtypeStruct((2, 8, LANES), F32),
            jax.ShapeDtypeStruct((groups, 8, LANES), F32),
        ),
        in_specs=[vmem()] * (count + 5),
        out_specs=(vmem(),) * 3,
        scratch_shapes=[pltpu.VMEM((2, steps, HALF), F32)],
        compiler_params=pltpu.CompilerParams(vmem_limit_bytes=MID),
        cost_estimate=cost(steps * LANES * 16, steps * LANES * (2 * count + 12)),
        name="local_recurrence",
    )(*parts, cr, ci, qr, qi, whole)


def history_kernel(got_ref, enter_ref, pre_ref, w_ref, qr_ref, qi_ref, history_ref, out_ref, hist_ref):
    inner = w_ref.shape[0]
    mine = lax.axis_index(TM)
    sr = jnp.zeros((1, LANES), F32)
    si = jnp.zeros((1, LANES), F32)
    for k in range(got_ref.shape[0] - 1):
        tile = got_ref[k]
        br, bi, ar, ai = (tile[r : r + 1, :] for r in range(4))
        nr = ar * sr - ai * si + br
        ni = ar * si + ai * sr + bi
        take = mine > k
        sr = jnp.where(take, nr, sr)
        si = jnp.where(take, ni, si)
    er = enter_ref[0] + pre_ref[0] * sr - pre_ref[1] * si
    ei = enter_ref[1] + pre_ref[0] * si + pre_ref[1] * sr
    for j in range(inner):
        value = w_ref[j] + qr_ref[j] * er - qi_ref[j] * ei
        for h in range(2):
            hist_ref[h, pl.ds(j, 8, stride=inner), :] = value[:, h * HALF : (h + 1) * HALF]
    natural = jnp.concatenate([hist_ref[h] for h in range(2)], axis=1)
    history_ref[...] = natural
    rounded = natural.astype(BF16)
    for k in range(out_ref.shape[0]):
        out_ref[k] = rounded


def make_history(got, enter, pre, w, qr, qi, copies):
    inner = w.shape[0]
    steps = inner * 8
    return pl.pallas_call(
        history_kernel,
        out_shape=(
            jax.ShapeDtypeStruct((steps, LANES), F32),
            jax.ShapeDtypeStruct((copies, steps, LANES), BF16),
        ),
        in_specs=[vmem()] * 6,
        out_specs=(vmem(), vmem()),
        scratch_shapes=[pltpu.VMEM((2, steps, HALF), F32)],
        compiler_params=pltpu.CompilerParams(vmem_limit_bytes=MID),
        cost_estimate=cost(steps * LANES * 4, steps * LANES * 18),
        name="make_history",
    )(got, enter, pre, w, qr, qi)


def turn_kernel(natural_ref, out_ref):
    for h in range(2):
        part = slice(h * HALF, (h + 1) * HALF)
        out_ref[part, :] = natural_ref[:, part].T


def turn_history(natural):
    steps, lanes = natural.shape
    return pl.pallas_call(
        turn_kernel,
        out_shape=jax.ShapeDtypeStruct((lanes, steps), F32),
        in_specs=[vmem()],
        out_specs=vmem(),
        compiler_params=pltpu.CompilerParams(vmem_limit_bytes=MID),
        cost_estimate=cost(steps * lanes, steps * lanes * 8),
        name="turn_history",
    )(natural)


def field_kernel(other, held_ref, shapes_ref, *refs):
    before, out_ref = refs[:-1], refs[-1]
    core = lax.axis_index("core")
    core = 1 - core if other else core
    wide = 512
    for n in range(0, out_ref.shape[1], wide):
        across = slice(n, n + wide)
        total = before[0][:, across] if before else None
        for q in range(held_ref.shape[0]):
            place = pl.multiple_of((2 * q + core) * LANES, LANES)
            part = jnp.dot(
                held_ref[q],
                shapes_ref[pl.ds(place, LANES), across],
                preferred_element_type=F32,
            )
            total = part if total is None else total + part
        out_ref[:, across] = total.astype(out_ref.dtype)


def add_field(other, held, staged, before=None):
    count, steps, _ = held.shape
    points = staged.shape[1]
    extra = [] if before is None else [before]
    return pl.pallas_call(
        lambda *refs: field_kernel(other, *refs),
        out_shape=jax.ShapeDtypeStruct((steps, points), F32 if before is None else BF16),
        in_specs=[vmem()] * (2 + len(extra)),
        out_specs=vmem(),
        compiler_params=pltpu.CompilerParams(vmem_limit_bytes=MID),
        cost_estimate=cost(2 * count * LANES * steps * points, 2 * count * LANES * points),
        name="add_field",
    )(held, staged, *extra)


def step_pairs(dx, dy):
    nx, ny = 4, 2
    return [
        (x * ny + y, (x + dx) % nx * ny + (y + dy) % ny) for x in range(nx) for y in range(ny)
    ]


def body(loads, phi, load_index, damping, frequency, gains, shapes):
    steps = loads.shape[0]
    inner = steps // 8
    groups = lax.axis_size(TM)
    pair = [(0, 1), (1, 0)]
    scat, sent, later, kept = open_partial(load_index.reshape(1, -1), loads, phi)
    first = lax.ppermute(sent, "core", pair)
    last = lax.ppermute(rest_partial(scat, later), "core", pair)
    parts = []
    for start, mates in ((0, first), (4, last)):
        for q, part in enumerate(more_partial(scat, kept, start, mates), start):
            here = STEPS[q] == (0, 0)
            parts.append(part if here else lax.ppermute(part, XY, step_pairs(*STEPS[q])))

    radius = jnp.exp(-damping)
    zr = (radius * jnp.cos(frequency)).reshape(1, -1)
    zi = (radius * jnp.sin(frequency)).reshape(1, -1)
    drive = jnp.sqrt(-jnp.expm1(-2.0 * damping)).reshape(1, -1)
    late, parts[7] = lax.optimization_barrier((shapes, parts[7]))
    *coef, staged = coefficients(gains.reshape(1, -1), zr, zi, drive, late)
    cr, ci, qr, qi, pre, whole = coef
    w, enter, payload = local_recurrence(parts, cr, ci, qr, qi, whole, groups)
    states = lax.all_to_all(payload, TM, 0, 0)
    natural, out = make_history(states, enter, pre, w, qr, qi, lax.axis_size(XY))
    near = lax.all_to_all(out, XY, 0, 0)
    natural, near = lax.optimization_barrier((natural, near))
    far = lax.ppermute(near, "core", pair)
    history = turn_history(natural)
    field = add_field(False, near, staged)
    field = add_field(True, far, staged, field)
    return field, history


def solution(mesh):
    grid = Mesh(mesh.devices.reshape(4, 2, 4, 2, 2), ("z", "yh", "x", "yl", "core"))
    placed = (
        P(TM, DOF),
        P(DOF, None),
        P(DOF),
        P(DOF),
        P(DOF),
        P(TM),
        P(None, DOF),
    )
    return jax.shard_map(
        body,
        mesh=grid,
        in_specs=placed,
        out_specs=(P(TM, DOF), P(DOF, TM)),
        check_vma=False,
    )
```

```python
import jax
import jax.numpy as jnp
from jax import lax
from jax.experimental import pallas as pl
from jax.experimental.pallas import tpu as pltpu
from jax.sharding import Mesh, PartitionSpec as P

TM = ("z", "yh")
XY = ("x", "yl")
DOF = ("x", "yl", "core")
F32 = jnp.float32
BF16 = jnp.bfloat16
LANES = 256
HALF = 128
MID = 12 * 1024 * 1024
DEEP = 256
EARLY = 2
STEPS = ((2, 1), (1, 1), (3, 0), (2, 0), (0, 1), (1, 0), (3, 1), (0, 0))


def vmem():
    return pl.BlockSpec(memory_space=pltpu.VMEM)


def cost(flops, moved):
    return pl.CostEstimate(flops=int(flops), bytes_accessed=int(moved), transcendentals=0)


def smem():
    return pl.BlockSpec(memory_space=pltpu.SMEM)


def hbm():
    return pl.BlockSpec(memory_space=pltpu.HBM)


def in_hbm(value):
    return pltpu.with_memory_space_constraint(value, pltpu.HBM)


def block_of(step, sign, other):
    dx, dy = step
    x = lax.rem(lax.axis_index("x") + (4 + sign * dx) % 4, 4)
    y = lax.rem(lax.axis_index("yl") + dy, 2)
    core = lax.axis_index("core")
    core = 1 - core if other else core
    return pl.multiple_of((2 * (2 * x + y) + core) * LANES, LANES)


def products(scat_ref, phi_ref, steps, other, wait=None):
    places = [block_of(step, 1, other) for step in steps]
    total = None
    for k in range(0, phi_ref.shape[0], DEEP):
        if wait is not None:
            wait(k // DEEP)
        rows = slice(k, k + DEEP)
        block = jnp.concatenate([phi_ref[rows, pl.ds(place, LANES)] for place in places], axis=1)
        part = jnp.dot(scat_ref[:, rows], block, preferred_element_type=F32)
        total = part if total is None else total + part
    return [total[:, q * LANES : (q + 1) * LANES] for q in range(len(steps))]


def open_kernel(index_hbm, loads_hbm, phi_hbm, scat_ref, sent_ref, phi_ref,
                index_ref, loads_ref, sems, load_sems):
    index_copy = pltpu.make_async_copy(index_hbm, index_ref, load_sems.at[0])
    loads_copy = pltpu.make_async_copy(loads_hbm, loads_ref, load_sems.at[1])
    copies = []
    for q in range(phi_ref.shape[0] // DEEP):
        part = pl.ds(q * DEEP, DEEP)
        copies.append(pltpu.make_async_copy(phi_hbm.at[part], phi_ref.at[part], sems.at[q]))
    for copy in [index_copy, loads_copy] + copies:
        copy.start()
    rows = scat_ref.shape[1]
    channels = index_ref.shape[1]
    place = lax.broadcasted_iota(jnp.int32, (rows, channels), 0)
    index_copy.wait()
    local = index_ref[...] - lax.axis_index(DOF) * rows
    onehot = jnp.where(place == local, 1.0, 0.0).astype(BF16)
    loads_copy.wait()
    summed = lax.dot_general(
        loads_ref[...], onehot, (((1,), (1,)), ((), ())), preferred_element_type=F32
    )
    scat_ref[...] = summed.astype(BF16)
    mine = products(scat_ref, phi_ref, STEPS[:EARLY], True, lambda k: copies[k].wait())
    for q, value in enumerate(mine):
        sent_ref[q] = value.astype(BF16)


def open_partial(index_row, loads, phi):
    steps, channels = loads.shape
    rows = phi.shape[0]
    return pl.pallas_call(
        open_kernel,
        out_shape=(
            pltpu.VMEM((steps, rows), BF16),
            jax.ShapeDtypeStruct((EARLY, steps, LANES), BF16),
            pltpu.VMEM(phi.shape, BF16),
        ),
        in_specs=[hbm(), hbm(), hbm()],
        out_specs=(vmem(),) * 3,
        scratch_shapes=[
            pltpu.VMEM((1, channels), jnp.int32),
            pltpu.VMEM((steps, channels), BF16),
            pltpu.SemaphoreType.DMA((rows // DEEP,)),
            pltpu.SemaphoreType.DMA((2,)),
        ],
        cost_estimate=cost(2 * steps * rows * (channels + EARLY * LANES), 32 * rows * LANES),
        compiler_params=pltpu.CompilerParams(vmem_limit_bytes=MID),
        name="open_partial",
    )(in_hbm(index_row), in_hbm(loads), in_hbm(phi))


def rest_kernel(scat_ref, phi_ref, sent_ref):
    for q, value in enumerate(products(scat_ref, phi_ref, STEPS[EARLY:], True)):
        sent_ref[q] = value.astype(BF16)


def rest_partial(scat, phi):
    steps, rows = scat.shape
    return pl.pallas_call(
        rest_kernel,
        out_shape=jax.ShapeDtypeStruct((8 - EARLY, steps, LANES), BF16),
        in_specs=[vmem(), vmem()],
        out_specs=vmem(),
        cost_estimate=cost(8 * steps * rows * LANES, 8 * rows * LANES),
        compiler_params=pltpu.CompilerParams(vmem_limit_bytes=MID),
        name="rest_partial",
    )(scat, phi)


def more_kernel(chosen, scat_ref, phi_ref, got_ref, *outs):
    for q, value in enumerate(products(scat_ref, phi_ref, chosen, False)):
        outs[q][...] = (value + got_ref[q].astype(F32)).astype(BF16)


def more_partial(scat, phi, chosen, got):
    steps, rows = scat.shape
    count = len(chosen)
    return pl.pallas_call(
        lambda *refs: more_kernel(chosen, *refs),
        out_shape=(jax.ShapeDtypeStruct((steps, LANES), BF16),) * count,
        in_specs=[vmem()] * 3,
        out_specs=(vmem(),) * count,
        cost_estimate=cost(2 * count * steps * rows * LANES, 2 * count * rows * LANES),
        compiler_params=pltpu.CompilerParams(vmem_limit_bytes=MID),
        name="more_partial",
    )(scat, phi, got)


def coef_kernel(gains_ref, zr_ref, zi_ref, drive_ref, shapes_ref,
                cr_ref, ci_ref, qr_ref, qi_ref, pre_ref, whole_ref, staged_ref, sems):
    tall = staged_ref.shape[0] // 8
    copies = []
    for q in range(8):
        part = pl.ds(q * tall, tall)
        copies.append(pltpu.make_async_copy(shapes_ref.at[part], staged_ref.at[part], sems.at[q]))
    for copy in copies:
        copy.start()
    steps = gains_ref.shape[1]
    inner = steps // 8
    row = lax.broadcasted_iota(jnp.int32, (steps, steps), 0)
    wanted = lax.rem(row, 8) * inner + lax.div(row, 8)
    hit = lax.broadcasted_iota(jnp.int32, (steps, steps), 1) == wanted
    left = gains_ref[...]
    gain_all = jnp.zeros((steps, LANES), F32)
    ones = jnp.ones((steps, LANES), BF16)
    for _ in range(3):
        term = left.astype(BF16)
        left = left - term.astype(F32)
        chosen = jnp.where(hit, term.astype(F32), 0.0).astype(BF16)
        gain_all = gain_all + jnp.dot(chosen, ones, preferred_element_type=F32)
    zr = zr_ref[...]
    zi = zi_ref[...]
    qr = jnp.ones((8, LANES), F32)
    qi = jnp.zeros((8, LANES), F32)
    for j in range(inner):
        gain = gain_all[8 * j : 8 * j + 8, :]
        cr = gain * zr
        ci = gain * zi
        cr_ref[j] = cr
        ci_ref[j] = ci
        qr, qi = qr * cr - qi * ci, qr * ci + qi * cr
        qr_ref[j] = qr
        qi_ref[j] = qi
    pr = jnp.ones((1, LANES), F32)
    pi = jnp.zeros((1, LANES), F32)
    for b in range(8):
        pre_ref[0, b : b + 1, :] = pr
        pre_ref[1, b : b + 1, :] = pi
        br = qr[b : b + 1, :]
        bi = qi[b : b + 1, :]
        pr, pi = pr * br - pi * bi, pr * bi + pi * br
    whole_ref[0:1, :] = pr
    whole_ref[1:2, :] = pi
    whole_ref[2:3, :] = drive_ref[...]
    whole_ref[3:8, :] = jnp.zeros((5, LANES), F32)
    for copy in copies:
        copy.wait()


def coefficients(gains, zr, zi, drive, shapes):
    inner = gains.shape[1] // 8
    full = jax.ShapeDtypeStruct((inner, 8, LANES), F32)
    return pl.pallas_call(
        coef_kernel,
        out_shape=(
            full,
            full,
            full,
            full,
            jax.ShapeDtypeStruct((2, 8, LANES), F32),
            jax.ShapeDtypeStruct((8, LANES), F32),
            pltpu.VMEM(shapes.shape, shapes.dtype),
        ),
        in_specs=[vmem()] * 4 + [hbm()],
        out_specs=(vmem(),) * 7,
        scratch_shapes=[pltpu.SemaphoreType.DMA((8,))],
        cost_estimate=cost(inner * 64 * LANES, 2 * shapes.size),
        compiler_params=pltpu.CompilerParams(vmem_limit_bytes=MID),
        name="coefficients",
    )(gains, zr, zi, drive, in_hbm(shapes))


def local_kernel(*refs):
    parts = refs[:-9]
    cr_ref, ci_ref, qr_ref, qi_ref, whole_ref, w_ref, enter_ref, send_ref, push_ref = refs[-9:]
    steps = parts[0].shape[0]
    inner = steps // 8
    drive = whole_ref[2:3, :]
    tile = 64
    for s in range(0, steps, tile):
        total = parts[0][s : s + tile, :].astype(F32)
        for part in parts[1:]:
            total += part[s : s + tile, :].astype(F32)
        total = total * drive
        for h in range(2):
            push_ref[h, s : s + tile, :] = total[:, h * HALF : (h + 1) * HALF]
    wr = jnp.zeros((8, LANES), F32)
    wi = jnp.zeros((8, LANES), F32)
    for j in range(inner):
        push = jnp.concatenate(
            [push_ref[h, pl.ds(j, 8, stride=inner), :] for h in range(2)], axis=1
        )
        cr = cr_ref[j]
        ci = ci_ref[j]
        wr, wi = cr * wr - ci * wi + push, cr * wi + ci * wr
        w_ref[j] = wr
    qr = qr_ref[inner - 1]
    qi = qi_ref[inner - 1]
    sr = jnp.zeros((1, LANES), F32)
    si = jnp.zeros((1, LANES), F32)
    for b in range(8):
        enter_ref[0, b : b + 1, :] = sr
        enter_ref[1, b : b + 1, :] = si
        br = qr[b : b + 1, :]
        bi = qi[b : b + 1, :]
        sr, si = (
            br * sr - bi * si + wr[b : b + 1, :],
            br * si + bi * sr + wi[b : b + 1, :],
        )
    row = lax.broadcasted_iota(jnp.int32, (8, LANES), 0)
    tile = jnp.where(row == 0, sr, jnp.where(row == 1, si, 0.0))
    tile = jnp.where(row == 2, whole_ref[0:1, :], jnp.where(row == 3, whole_ref[1:2, :], tile))
    for k in range(send_ref.shape[0]):
        send_ref[k] = tile


def local_recurrence(parts, cr, ci, qr, qi, whole, groups):
    count, steps = len(parts), parts[0].shape[0]
    inner = steps // 8
    return pl.pallas_call(
        local_kernel,
        out_shape=(
            jax.ShapeDtypeStruct((inner, 8, LANES), F32),
            jax.ShapeDtypeStruct((2, 8, LANES), F32),
            jax.ShapeDtypeStruct((groups, 8, LANES), F32),
        ),
        in_specs=[vmem()] * (count + 5),
        out_specs=(vmem(),) * 3,
        scratch_shapes=[pltpu.VMEM((2, steps, HALF), F32)],
        compiler_params=pltpu.CompilerParams(vmem_limit_bytes=MID),
        cost_estimate=cost(steps * LANES * 16, steps * LANES * (2 * count + 12)),
        name="local_recurrence",
    )(*parts, cr, ci, qr, qi, whole)


def history_kernel(got_ref, enter_ref, pre_ref, w_ref, qr_ref, qi_ref, history_ref, out_ref, hist_ref):
    inner = w_ref.shape[0]
    mine = lax.axis_index(TM)
    sr = jnp.zeros((1, LANES), F32)
    si = jnp.zeros((1, LANES), F32)
    for k in range(got_ref.shape[0] - 1):
        tile = got_ref[k]
        br, bi, ar, ai = (tile[r : r + 1, :] for r in range(4))
        nr = ar * sr - ai * si + br
        ni = ar * si + ai * sr + bi
        take = mine > k
        sr = jnp.where(take, nr, sr)
        si = jnp.where(take, ni, si)
    er = enter_ref[0] + pre_ref[0] * sr - pre_ref[1] * si
    ei = enter_ref[1] + pre_ref[0] * si + pre_ref[1] * sr
    for j in range(inner):
        value = w_ref[j] + qr_ref[j] * er - qi_ref[j] * ei
        for h in range(2):
            hist_ref[h, pl.ds(j, 8, stride=inner), :] = value[:, h * HALF : (h + 1) * HALF]
    natural = jnp.concatenate([hist_ref[h] for h in range(2)], axis=1)
    history_ref[...] = natural
    rounded = natural.astype(BF16)
    for k in range(out_ref.shape[0]):
        out_ref[k] = rounded


def make_history(got, enter, pre, w, qr, qi, copies):
    inner = w.shape[0]
    steps = inner * 8
    return pl.pallas_call(
        history_kernel,
        out_shape=(
            jax.ShapeDtypeStruct((steps, LANES), F32),
            jax.ShapeDtypeStruct((copies, steps, LANES), BF16),
        ),
        in_specs=[vmem()] * 6,
        out_specs=(vmem(), vmem()),
        scratch_shapes=[pltpu.VMEM((2, steps, HALF), F32)],
        compiler_params=pltpu.CompilerParams(vmem_limit_bytes=MID),
        cost_estimate=cost(steps * LANES * 4, steps * LANES * 18),
        name="make_history",
    )(got, enter, pre, w, qr, qi)


WIDE = 512


def field_tiles(other, held_ref, before, shapes_ref, store):
    core = lax.axis_index("core")
    core = 1 - core if other else core
    for n in range(0, shapes_ref.shape[1], WIDE):
        across = slice(n, n + WIDE)
        total = before[0][:, across] if before else None
        for q in range(held_ref.shape[0]):
            place = pl.multiple_of((2 * q + core) * LANES, LANES)
            product = jnp.dot(
                held_ref[q], shapes_ref[pl.ds(place, LANES), across], preferred_element_type=F32
            )
            total = product if total is None else total + product
        store(n, total)


def near_kernel(held_ref, shapes_ref, natural_ref, out_ref, history_ref):
    piece = HALF

    def store(n, total):
        out_ref[:, n : n + WIDE] = total
        first = n // WIDE * piece
        if first < natural_ref.shape[0]:
            part = slice(first, first + piece)
            for h in range(2):
                lanes = slice(h * HALF, (h + 1) * HALF)
                history_ref[lanes, part] = natural_ref[part, lanes].T

    field_tiles(False, held_ref, [], shapes_ref, store)


def far_kernel(held_ref, shapes_ref, before_ref, out_hbm, out_ref, sems):
    copies = []

    def store(n, total):
        out_ref[:, n : n + WIDE] = total.astype(BF16)
        across = pl.ds(n, WIDE)
        copy = pltpu.make_async_copy(
            out_ref.at[:, across], out_hbm.at[:, across], sems.at[n // WIDE]
        )
        copy.start()
        copies.append(copy)

    field_tiles(True, held_ref, [before_ref], shapes_ref, store)
    for copy in copies:
        copy.wait()


def near_field(held, staged, natural):
    count, steps, lanes = held.shape
    points = staged.shape[1]
    return pl.pallas_call(
        near_kernel,
        out_shape=(
            jax.ShapeDtypeStruct((steps, points), F32),
            jax.ShapeDtypeStruct((lanes, steps), F32),
        ),
        in_specs=[vmem()] * 3,
        out_specs=(vmem(), vmem()),
        compiler_params=pltpu.CompilerParams(vmem_limit_bytes=MID),
        cost_estimate=cost(2 * count * LANES * steps * points, 2 * count * LANES * points),
        name="near_field",
    )(held, staged, natural)


def far_field(held, staged, before):
    count, steps, _ = held.shape
    points = staged.shape[1]
    return pl.pallas_call(
        far_kernel,
        out_shape=jax.ShapeDtypeStruct((steps, points), BF16),
        in_specs=[vmem()] * 3,
        out_specs=hbm(),
        scratch_shapes=[
            pltpu.VMEM((steps, points), BF16),
            pltpu.SemaphoreType.DMA((points // WIDE,)),
        ],
        compiler_params=pltpu.CompilerParams(vmem_limit_bytes=MID),
        cost_estimate=cost(2 * count * LANES * steps * points, 2 * count * LANES * points),
        name="far_field",
    )(held, staged, before)


def step_pairs(dx, dy):
    nx, ny = 4, 2
    return [
        (x * ny + y, (x + dx) % nx * ny + (y + dy) % ny) for x in range(nx) for y in range(ny)
    ]


def body(loads, phi, load_index, damping, frequency, gains, shapes):
    steps = loads.shape[0]
    inner = steps // 8
    groups = lax.axis_size(TM)
    pair = [(0, 1), (1, 0)]
    scat, sent, held_phi = open_partial(load_index.reshape(1, -1), loads, phi)
    first = lax.ppermute(sent, "core", pair)
    sent = rest_partial(scat, held_phi)
    summed = list(more_partial(scat, held_phi, STEPS[:EARLY], first))
    sent, *summed = lax.optimization_barrier((sent, *summed))
    last = lax.ppermute(sent, "core", pair)
    summed += more_partial(scat, held_phi, STEPS[EARLY:], last)
    parts = []
    for step, part in zip(STEPS, summed):
        parts.append(part if step == (0, 0) else lax.ppermute(part, XY, step_pairs(*step)))

    radius = jnp.exp(-damping)
    zr = (radius * jnp.cos(frequency)).reshape(1, -1)
    zi = (radius * jnp.sin(frequency)).reshape(1, -1)
    drive = jnp.sqrt(-jnp.expm1(-2.0 * damping)).reshape(1, -1)
    late, parts[7] = lax.optimization_barrier((shapes, parts[7]))
    *coef, staged = coefficients(gains.reshape(1, -1), zr, zi, drive, late)
    cr, ci, qr, qi, pre, whole = coef
    w, enter, payload = local_recurrence(parts, cr, ci, qr, qi, whole, groups)
    states = lax.all_to_all(payload, TM, 0, 0)
    natural, out = make_history(states, enter, pre, w, qr, qi, lax.axis_size(XY))
    near = lax.all_to_all(out, XY, 0, 0)
    far = lax.ppermute(near, "core", pair)
    field, history = near_field(near, staged, natural)
    return far_field(far, staged, field), history


def solution(mesh):
    grid = Mesh(mesh.devices.reshape(4, 2, 4, 2, 2), ("z", "yh", "x", "yl", "core"))
    placed = (
        P(TM, DOF),
        P(DOF, None),
        P(DOF),
        P(DOF),
        P(DOF),
        P(TM),
        P(None, DOF),
    )
    return jax.shard_map(
        body,
        mesh=grid,
        in_specs=placed,
        out_specs=(P(TM, DOF), P(DOF, TM)),
        check_vma=False,
    )
```

```python
import jax
import jax.numpy as jnp
from jax import lax
from jax.experimental import pallas as pl
from jax.experimental.pallas import tpu as pltpu
from jax.sharding import Mesh, PartitionSpec as P

TM = ("z", "yh")
XY = ("x", "yl")
DOF = ("x", "yl", "core")
F32 = jnp.float32
BF16 = jnp.bfloat16
LANES = 256
HALF = 128
MID = 12 * 1024 * 1024
DEEP = 256
EARLY = 2
FLOPS = 500 * 1000 * 1000
STEPS = ((2, 1), (1, 1), (3, 0), (2, 0), (0, 1), (1, 0), (3, 1), (0, 0))
SPREAD = ((2, 0), (2, 1), (1, 0), (0, 1), (3, 1), (1, 1), (3, 0))


def vmem():
    return pl.BlockSpec(memory_space=pltpu.VMEM)


def cost(flops, moved):
    return pl.CostEstimate(flops=int(flops), bytes_accessed=int(moved), transcendentals=0)


def smem():
    return pl.BlockSpec(memory_space=pltpu.SMEM)


def hbm():
    return pl.BlockSpec(memory_space=pltpu.HBM)


def in_hbm(value):
    return pltpu.with_memory_space_constraint(value, pltpu.HBM)


def block_of(step, sign, other):
    dx, dy = step
    x = lax.rem(lax.axis_index("x") + (4 + sign * dx) % 4, 4)
    y = lax.rem(lax.axis_index("yl") + dy, 2)
    core = lax.axis_index("core")
    core = 1 - core if other else core
    return pl.multiple_of((2 * (2 * x + y) + core) * LANES, LANES)


def products(scat_ref, phi_ref, steps, other, wait=None):
    places = [block_of(step, 1, other) for step in steps]
    total = None
    for k in range(0, phi_ref.shape[0], DEEP):
        if wait is not None:
            wait(k // DEEP)
        rows = slice(k, k + DEEP)
        block = jnp.concatenate([phi_ref[rows, pl.ds(place, LANES)] for place in places], axis=1)
        part = jnp.dot(scat_ref[:, rows], block, preferred_element_type=F32)
        total = part if total is None else total + part
    return [total[:, q * LANES : (q + 1) * LANES] for q in range(len(steps))]


def open_kernel(index_hbm, loads_hbm, phi_hbm, scat_ref, sent_ref, phi_ref,
                index_ref, loads_ref, sems, load_sems):
    index_copy = pltpu.make_async_copy(index_hbm, index_ref, load_sems.at[0])
    loads_copy = pltpu.make_async_copy(loads_hbm, loads_ref, load_sems.at[1])
    copies = []
    for q in range(phi_ref.shape[0] // DEEP):
        part = pl.ds(q * DEEP, DEEP)
        copies.append(pltpu.make_async_copy(phi_hbm.at[part], phi_ref.at[part], sems.at[q]))
    for copy in [index_copy, loads_copy] + copies:
        copy.start()
    rows = scat_ref.shape[1]
    channels = index_ref.shape[1]
    place = lax.broadcasted_iota(jnp.int32, (channels, rows), 1).astype(F32)
    index_copy.wait()
    local = (index_ref[...] - lax.axis_index(DOF) * rows).astype(F32)
    column = jnp.broadcast_to(local, (8, channels)).T[:, 0:1]
    onehot = jnp.where(place == column, 1.0, 0.0).astype(BF16)
    loads_copy.wait()
    summed = jnp.dot(loads_ref[...], onehot, preferred_element_type=F32)
    scat_ref[...] = summed.astype(BF16)
    mine = products(scat_ref, phi_ref, STEPS[:EARLY], True, lambda k: copies[k].wait())
    for q, value in enumerate(mine):
        sent_ref[q] = value.astype(BF16)


def open_partial(index_row, loads, phi):
    steps, channels = loads.shape
    rows = phi.shape[0]
    return pl.pallas_call(
        open_kernel,
        out_shape=(
            pltpu.VMEM((steps, rows), BF16),
            jax.ShapeDtypeStruct((EARLY, steps, LANES), BF16),
            pltpu.VMEM(phi.shape, BF16),
        ),
        in_specs=[hbm(), hbm(), hbm()],
        out_specs=(vmem(),) * 3,
        scratch_shapes=[
            pltpu.VMEM((1, channels), jnp.int32),
            pltpu.VMEM((steps, channels), BF16),
            pltpu.SemaphoreType.DMA((rows // DEEP,)),
            pltpu.SemaphoreType.DMA((2,)),
        ],
        cost_estimate=cost(2 * steps * rows * (channels + EARLY * LANES), 32 * rows * LANES),
        compiler_params=pltpu.CompilerParams(vmem_limit_bytes=MID),
        name="open_partial",
    )(in_hbm(index_row), in_hbm(loads), in_hbm(phi))


def rest_kernel(scat_ref, phi_ref, sent_ref):
    for q, value in enumerate(products(scat_ref, phi_ref, STEPS[EARLY:], True)):
        sent_ref[q] = value.astype(BF16)


def rest_partial(scat, phi):
    steps, rows = scat.shape
    return pl.pallas_call(
        rest_kernel,
        out_shape=jax.ShapeDtypeStruct((8 - EARLY, steps, LANES), BF16),
        in_specs=[vmem(), vmem()],
        out_specs=vmem(),
        cost_estimate=cost(8 * steps * rows * LANES, 8 * rows * LANES),
        compiler_params=pltpu.CompilerParams(vmem_limit_bytes=MID),
        name="rest_partial",
    )(scat, phi)


def more_kernel(chosen, scat_ref, phi_ref, got_ref, *outs):
    for q, value in enumerate(products(scat_ref, phi_ref, chosen, False)):
        outs[q][...] = (value + got_ref[q].astype(F32)).astype(BF16)


def more_partial(scat, phi, chosen, got):
    steps, rows = scat.shape
    count = len(chosen)
    return pl.pallas_call(
        lambda *refs: more_kernel(chosen, *refs),
        out_shape=(jax.ShapeDtypeStruct((steps, LANES), BF16),) * count,
        in_specs=[vmem()] * 3,
        out_specs=(vmem(),) * count,
        cost_estimate=cost(2 * count * steps * rows * LANES, 2 * count * rows * LANES),
        compiler_params=pltpu.CompilerParams(vmem_limit_bytes=MID),
        name="more_partial",
    )(scat, phi, got)


def coef_kernel(gains_ref, zr_ref, zi_ref, drive_ref, shapes_ref,
                cr_ref, ci_ref, qr_ref, qi_ref, pre_ref, whole_ref, staged_ref, sems):
    tall = staged_ref.shape[0] // 8
    copies = []
    for q in range(8):
        part = pl.ds(q * tall, tall)
        copies.append(pltpu.make_async_copy(shapes_ref.at[part], staged_ref.at[part], sems.at[q]))
    for copy in copies:
        copy.start()
    steps = gains_ref.shape[1]
    inner = steps // 8
    row = lax.broadcasted_iota(jnp.int32, (steps, steps), 0)
    wanted = lax.rem(row, 8) * inner + lax.div(row, 8)
    hit = lax.broadcasted_iota(jnp.int32, (steps, steps), 1) == wanted
    left = gains_ref[...]
    gain_all = jnp.zeros((steps, LANES), F32)
    ones = jnp.ones((steps, LANES), BF16)
    for _ in range(3):
        term = left.astype(BF16)
        left = left - term.astype(F32)
        chosen = jnp.where(hit, term.astype(F32), 0.0).astype(BF16)
        gain_all = gain_all + jnp.dot(chosen, ones, preferred_element_type=F32)
    zr = zr_ref[...]
    zi = zi_ref[...]
    qr = jnp.ones((8, LANES), F32)
    qi = jnp.zeros((8, LANES), F32)
    for j in range(inner):
        gain = gain_all[8 * j : 8 * j + 8, :]
        cr = gain * zr
        ci = gain * zi
        cr_ref[j] = cr
        ci_ref[j] = ci
        qr, qi = qr * cr - qi * ci, qr * ci + qi * cr
        qr_ref[j] = qr
        qi_ref[j] = qi
    pr = jnp.ones((1, LANES), F32)
    pi = jnp.zeros((1, LANES), F32)
    for b in range(8):
        pre_ref[0, b : b + 1, :] = pr
        pre_ref[1, b : b + 1, :] = pi
        br = qr[b : b + 1, :]
        bi = qi[b : b + 1, :]
        pr, pi = pr * br - pi * bi, pr * bi + pi * br
    whole_ref[0:1, :] = pr
    whole_ref[1:2, :] = pi
    whole_ref[2:3, :] = drive_ref[...]
    whole_ref[3:8, :] = jnp.zeros((5, LANES), F32)
    for copy in copies:
        copy.wait()


def coefficients(gains, zr, zi, drive, shapes):
    inner = gains.shape[1] // 8
    full = jax.ShapeDtypeStruct((inner, 8, LANES), F32)
    return pl.pallas_call(
        coef_kernel,
        out_shape=(
            full,
            full,
            full,
            full,
            jax.ShapeDtypeStruct((2, 8, LANES), F32),
            jax.ShapeDtypeStruct((8, LANES), F32),
            pltpu.VMEM(shapes.shape, shapes.dtype),
        ),
        in_specs=[vmem()] * 4 + [hbm()],
        out_specs=(vmem(),) * 7,
        scratch_shapes=[pltpu.SemaphoreType.DMA((8,))],
        cost_estimate=cost(inner * 64 * LANES, 2 * shapes.size),
        compiler_params=pltpu.CompilerParams(vmem_limit_bytes=MID),
        name="coefficients",
    )(gains, zr, zi, drive, in_hbm(shapes))


def local_kernel(*refs):
    parts = refs[:-9]
    cr_ref, ci_ref, qr_ref, qi_ref, whole_ref, w_ref, enter_ref, send_ref, push_ref = refs[-9:]
    steps = parts[0].shape[0]
    inner = steps // 8
    drive = whole_ref[2:3, :]
    tile = 64
    for s in range(0, steps, tile):
        total = parts[0][s : s + tile, :].astype(F32)
        for part in parts[1:]:
            total += part[s : s + tile, :].astype(F32)
        total = total * drive
        for h in range(2):
            push_ref[h, s : s + tile, :] = total[:, h * HALF : (h + 1) * HALF]
    wr = jnp.zeros((8, LANES), F32)
    wi = jnp.zeros((8, LANES), F32)
    for j in range(inner):
        push = jnp.concatenate(
            [push_ref[h, pl.ds(j, 8, stride=inner), :] for h in range(2)], axis=1
        )
        cr = cr_ref[j]
        ci = ci_ref[j]
        wr, wi = cr * wr - ci * wi + push, cr * wi + ci * wr
        w_ref[j] = wr
    qr = qr_ref[inner - 1]
    qi = qi_ref[inner - 1]
    sr = jnp.zeros((1, LANES), F32)
    si = jnp.zeros((1, LANES), F32)
    for b in range(8):
        enter_ref[0, b : b + 1, :] = sr
        enter_ref[1, b : b + 1, :] = si
        br = qr[b : b + 1, :]
        bi = qi[b : b + 1, :]
        sr, si = (
            br * sr - bi * si + wr[b : b + 1, :],
            br * si + bi * sr + wi[b : b + 1, :],
        )
    row = lax.broadcasted_iota(jnp.int32, (8, LANES), 0)
    tile = jnp.where(row == 0, sr, jnp.where(row == 1, si, 0.0))
    tile = jnp.where(row == 2, whole_ref[0:1, :], jnp.where(row == 3, whole_ref[1:2, :], tile))
    for k in range(send_ref.shape[0]):
        send_ref[k] = tile


def local_recurrence(parts, cr, ci, qr, qi, whole, groups):
    count, steps = len(parts), parts[0].shape[0]
    inner = steps // 8
    return pl.pallas_call(
        local_kernel,
        out_shape=(
            jax.ShapeDtypeStruct((inner, 8, LANES), F32),
            jax.ShapeDtypeStruct((2, 8, LANES), F32),
            jax.ShapeDtypeStruct((groups, 8, LANES), F32),
        ),
        in_specs=[vmem()] * (count + 5),
        out_specs=(vmem(),) * 3,
        scratch_shapes=[pltpu.VMEM((2, steps, HALF), F32)],
        compiler_params=pltpu.CompilerParams(vmem_limit_bytes=MID),
        cost_estimate=cost(steps * LANES * 16, steps * LANES * (2 * count + 12)),
        name="local_recurrence",
    )(*parts, cr, ci, qr, qi, whole)


def history_kernel(got_ref, enter_ref, pre_ref, w_ref, qr_ref, qi_ref, history_ref, out_ref, hist_ref):
    inner = w_ref.shape[0]
    mine = lax.axis_index(TM)
    sr = jnp.zeros((1, LANES), F32)
    si = jnp.zeros((1, LANES), F32)
    for k in range(got_ref.shape[0] - 1):
        tile = got_ref[k]
        br, bi, ar, ai = (tile[r : r + 1, :] for r in range(4))
        nr = ar * sr - ai * si + br
        ni = ar * si + ai * sr + bi
        take = mine > k
        sr = jnp.where(take, nr, sr)
        si = jnp.where(take, ni, si)
    er = enter_ref[0] + pre_ref[0] * sr - pre_ref[1] * si
    ei = enter_ref[1] + pre_ref[0] * si + pre_ref[1] * sr
    for j in range(inner):
        value = w_ref[j] + qr_ref[j] * er - qi_ref[j] * ei
        for h in range(2):
            hist_ref[h, pl.ds(j, 8, stride=inner), :] = value[:, h * HALF : (h + 1) * HALF]
    natural = jnp.concatenate([hist_ref[h] for h in range(2)], axis=1)
    history_ref[...] = natural
    rounded = natural.astype(BF16)
    out_ref[...] = rounded


def make_history(got, enter, pre, w, qr, qi):
    inner = w.shape[0]
    steps = inner * 8
    return pl.pallas_call(
        history_kernel,
        out_shape=(
            jax.ShapeDtypeStruct((steps, LANES), F32),
            jax.ShapeDtypeStruct((steps, LANES), BF16),
        ),
        in_specs=[vmem()] * 6,
        out_specs=(vmem(), vmem()),
        scratch_shapes=[pltpu.VMEM((2, steps, HALF), F32)],
        compiler_params=pltpu.CompilerParams(vmem_limit_bytes=MID),
        cost_estimate=cost(steps * LANES * 4, steps * LANES * 18),
        name="make_history",
    )(got, enter, pre, w, qr, qi)


WIDE = 512


def field_tiles(whose, held, before, shapes_ref, store):
    places = [block_of(step, -1, other) for step, other in whose]
    for n in range(0, shapes_ref.shape[1], WIDE):
        across = slice(n, n + WIDE)
        total = before[0][:, across] if before else None
        for place, part in zip(places, held):
            product = jnp.dot(
                part[...], shapes_ref[pl.ds(place, LANES), across], preferred_element_type=F32
            )
            total = product if total is None else total + product
        store(n, total)


def first_kernel(whose, shapes_ref, natural_ref, *refs):
    held, (out_ref, history_ref) = refs[:-2], refs[-2:]

    def store(n, total):
        out_ref[:, n : n + WIDE] = total
        first = n // WIDE * HALF
        if first < natural_ref.shape[0]:
            part = slice(first, first + HALF)
            for h in range(2):
                lanes = slice(h * HALF, (h + 1) * HALF)
                history_ref[lanes, part] = natural_ref[part, lanes].T

    field_tiles(whose, held, [], shapes_ref, store)


def first_field(whose, held, staged, natural):
    steps, lanes = natural.shape
    points = staged.shape[1]
    return pl.pallas_call(
        lambda *refs: first_kernel(whose, *refs),
        out_shape=(
            jax.ShapeDtypeStruct((steps, points), F32),
            jax.ShapeDtypeStruct((lanes, steps), F32),
        ),
        in_specs=[vmem()] * (2 + len(held)),
        out_specs=(vmem(),) * 2,
        compiler_params=pltpu.CompilerParams(vmem_limit_bytes=MID),
        cost_estimate=cost(FLOPS * len(held), FLOPS),
        name="first_field",
    )(staged, natural, *held)


def next_kernel(whose, shapes_ref, before_ref, *refs):
    def store(n, total):
        refs[-1][:, n : n + WIDE] = total

    field_tiles(whose, refs[:-1], [before_ref], shapes_ref, store)


def next_field(whose, held, staged, before):
    return pl.pallas_call(
        lambda *refs: next_kernel(whose, *refs),
        out_shape=jax.ShapeDtypeStruct(before.shape, F32),
        in_specs=[vmem()] * (2 + len(held)),
        out_specs=vmem(),
        compiler_params=pltpu.CompilerParams(vmem_limit_bytes=MID),
        cost_estimate=cost(FLOPS * len(whose), FLOPS),
        name="next_field",
    )(staged, before, *held)


def last_kernel(whose, shapes_ref, before_ref, *refs):
    held, (out_hbm, out_ref, sems) = refs[:-3], refs[-3:]
    copies = []

    def store(n, total):
        out_ref[:, n : n + WIDE] = total.astype(BF16)
        across = pl.ds(n, WIDE)
        copy = pltpu.make_async_copy(
            out_ref.at[:, across], out_hbm.at[:, across], sems.at[n // WIDE]
        )
        copy.start()
        copies.append(copy)

    field_tiles(whose, held, [before_ref], shapes_ref, store)
    for copy in copies:
        copy.wait()


def last_field(whose, held, staged, before):
    steps, points = before.shape
    return pl.pallas_call(
        lambda *refs: last_kernel(whose, *refs),
        out_shape=jax.ShapeDtypeStruct((steps, points), BF16),
        in_specs=[vmem()] * (2 + len(held)),
        out_specs=hbm(),
        scratch_shapes=[
            pltpu.VMEM((steps, points), BF16),
            pltpu.SemaphoreType.DMA((points // WIDE,)),
        ],
        compiler_params=pltpu.CompilerParams(vmem_limit_bytes=MID),
        cost_estimate=cost(FLOPS * len(whose), FLOPS),
        name="last_field",
    )(staged, before, *held)


def step_pairs(dx, dy):
    nx, ny = 4, 2
    return [
        (x * ny + y, (x + dx) % nx * ny + (y + dy) % ny) for x in range(nx) for y in range(ny)
    ]


def body(loads, phi, load_index, damping, frequency, gains, shapes):
    steps = loads.shape[0]
    inner = steps // 8
    groups = lax.axis_size(TM)
    pair = [(0, 1), (1, 0)]
    scat, sent, held_phi = open_partial(load_index.reshape(1, -1), loads, phi)
    first = lax.ppermute(sent, "core", pair)
    sent = rest_partial(scat, held_phi)
    summed = list(more_partial(scat, held_phi, STEPS[:EARLY], first))
    sent, *summed = lax.optimization_barrier((sent, *summed))
    last = lax.ppermute(sent, "core", pair)
    summed += more_partial(scat, held_phi, STEPS[EARLY:], last)
    parts = []
    for step, part in zip(STEPS, summed):
        parts.append(part if step == (0, 0) else lax.ppermute(part, XY, step_pairs(*step)))

    radius = jnp.exp(-damping)
    zr = (radius * jnp.cos(frequency)).reshape(1, -1)
    zi = (radius * jnp.sin(frequency)).reshape(1, -1)
    drive = jnp.sqrt(-jnp.expm1(-2.0 * damping)).reshape(1, -1)
    late, parts[7] = lax.optimization_barrier((shapes, parts[7]))
    *coef, staged = coefficients(gains.reshape(1, -1), zr, zi, drive, late)
    cr, ci, qr, qi, pre, whole = coef
    w, enter, payload = local_recurrence(parts, cr, ci, qr, qi, whole, groups)
    states = lax.all_to_all(payload, TM, 0, 0)
    natural, mine = make_history(states, enter, pre, w, qr, qi)
    near = [lax.ppermute(mine, XY, step_pairs(*step)) for step in SPREAD]
    near.append(mine)
    whose = [*SPREAD, (0, 0)]
    early = (3, 1)
    later = tuple(q for q in range(7) if q not in early)

    def pick(chosen):
        return [(whose[q], False) for q in chosen], [near[q] for q in chosen]

    field, history = first_field(*pick((7, *early)), staged, natural)
    sent = list(near)
    field, sent[0] = lax.optimization_barrier((field, sent[0]))
    far = [lax.ppermute(part, "core", pair) for part in sent]
    field = next_field(*pick(later), staged, field)
    field = last_field([(step, True) for step in whose], far, staged, field)
    return field, history


def solution(mesh):
    grid = Mesh(mesh.devices.reshape(4, 2, 4, 2, 2), ("z", "yh", "x", "yl", "core"))
    placed = (
        P(TM, DOF),
        P(DOF, None),
        P(DOF),
        P(DOF),
        P(DOF),
        P(TM),
        P(None, DOF),
    )
    return jax.shard_map(
        body,
        mesh=grid,
        in_specs=placed,
        out_specs=(P(TM, DOF), P(DOF, TM)),
        check_vma=False,
    )
```

```python
import jax
import jax.numpy as jnp
from jax import lax
from jax.experimental import pallas as pl
from jax.experimental.pallas import tpu as pltpu
from jax.sharding import Mesh, PartitionSpec as P

TM = ("z", "yh")
XY = ("x", "yl")
DOF = ("x", "yl", "core")
F32 = jnp.float32
BF16 = jnp.bfloat16
LANES = 256
HALF = 128
MID = 12 * 1024 * 1024
DEEP = 256
EARLY = 2
FLOPS = 500 * 1000 * 1000
STEPS = ((2, 1), (1, 1), (3, 0), (2, 0), (0, 1), (1, 0), (3, 1), (0, 0))
SPREAD = ((2, 0), (2, 1), (1, 0), (0, 1), (3, 1), (1, 1), (3, 0))


def vmem():
    return pl.BlockSpec(memory_space=pltpu.VMEM)


def cost(flops, moved):
    return pl.CostEstimate(flops=int(flops), bytes_accessed=int(moved), transcendentals=0)


def smem():
    return pl.BlockSpec(memory_space=pltpu.SMEM)


def hbm():
    return pl.BlockSpec(memory_space=pltpu.HBM)


def in_hbm(value):
    return pltpu.with_memory_space_constraint(value, pltpu.HBM)


def block_of(step, sign, other):
    dx, dy = step
    x = lax.rem(lax.axis_index("x") + (4 + sign * dx) % 4, 4)
    y = lax.rem(lax.axis_index("yl") + dy, 2)
    core = lax.axis_index("core")
    core = 1 - core if other else core
    return pl.multiple_of((2 * (2 * x + y) + core) * LANES, LANES)


def products(scat_ref, phi_ref, steps, other, wait=None):
    places = [block_of(step, 1, other) for step in steps]
    total = None
    for k in range(0, phi_ref.shape[0], DEEP):
        if wait is not None:
            wait(k // DEEP)
        rows = slice(k, k + DEEP)
        block = jnp.concatenate([phi_ref[rows, pl.ds(place, LANES)] for place in places], axis=1)
        part = jnp.dot(scat_ref[:, rows], block, preferred_element_type=F32)
        total = part if total is None else total + part
    return [total[:, q * LANES : (q + 1) * LANES] for q in range(len(steps))]


def open_kernel(index_hbm, loads_hbm, phi_hbm, scat_ref, sent_ref, phi_ref,
                index_ref, loads_ref, sems, load_sems):
    index_copy = pltpu.make_async_copy(index_hbm, index_ref, load_sems.at[0])
    loads_copy = pltpu.make_async_copy(loads_hbm, loads_ref, load_sems.at[1])
    copies = []
    for q in range(phi_ref.shape[0] // DEEP):
        part = pl.ds(q * DEEP, DEEP)
        copies.append(pltpu.make_async_copy(phi_hbm.at[part], phi_ref.at[part], sems.at[q]))
    for copy in [index_copy, loads_copy] + copies:
        copy.start()
    rows = scat_ref.shape[1]
    channels = index_ref.shape[1]
    place = lax.broadcasted_iota(jnp.int32, (channels, rows), 1).astype(F32)
    index_copy.wait()
    local = (index_ref[...] - lax.axis_index(DOF) * rows).astype(F32)
    column = jnp.broadcast_to(local, (8, channels)).T[:, 0:1]
    onehot = jnp.where(place == column, 1.0, 0.0).astype(BF16)
    loads_copy.wait()
    summed = jnp.dot(loads_ref[...], onehot, preferred_element_type=F32)
    scat_ref[...] = summed.astype(BF16)
    mine = products(scat_ref, phi_ref, STEPS[:EARLY], True, lambda k: copies[k].wait())
    for q, value in enumerate(mine):
        sent_ref[q] = value.astype(BF16)


def open_partial(index_row, loads, phi):
    steps, channels = loads.shape
    rows = phi.shape[0]
    return pl.pallas_call(
        open_kernel,
        out_shape=(
            pltpu.VMEM((steps, rows), BF16),
            jax.ShapeDtypeStruct((EARLY, steps, LANES), BF16),
            pltpu.VMEM(phi.shape, BF16),
        ),
        in_specs=[hbm(), hbm(), hbm()],
        out_specs=(vmem(),) * 3,
        scratch_shapes=[
            pltpu.VMEM((1, channels), jnp.int32),
            pltpu.VMEM((steps, channels), BF16),
            pltpu.SemaphoreType.DMA((rows // DEEP,)),
            pltpu.SemaphoreType.DMA((2,)),
        ],
        cost_estimate=cost(2 * steps * rows * (channels + EARLY * LANES), 32 * rows * LANES),
        compiler_params=pltpu.CompilerParams(vmem_limit_bytes=MID),
        name="open_partial",
    )(in_hbm(index_row), in_hbm(loads), in_hbm(phi))


def rest_kernel(scat_ref, phi_ref, sent_ref):
    for q, value in enumerate(products(scat_ref, phi_ref, STEPS[EARLY:], True)):
        sent_ref[q] = value.astype(BF16)


def rest_partial(scat, phi):
    steps, rows = scat.shape
    return pl.pallas_call(
        rest_kernel,
        out_shape=jax.ShapeDtypeStruct((8 - EARLY, steps, LANES), BF16),
        in_specs=[vmem(), vmem()],
        out_specs=vmem(),
        cost_estimate=cost(8 * steps * rows * LANES, 8 * rows * LANES),
        compiler_params=pltpu.CompilerParams(vmem_limit_bytes=MID),
        name="rest_partial",
    )(scat, phi)


def more_kernel(chosen, scat_ref, phi_ref, got_ref, *outs):
    for q, value in enumerate(products(scat_ref, phi_ref, chosen, False)):
        outs[q][...] = (value + got_ref[q].astype(F32)).astype(BF16)


def more_partial(scat, phi, chosen, got):
    steps, rows = scat.shape
    count = len(chosen)
    return pl.pallas_call(
        lambda *refs: more_kernel(chosen, *refs),
        out_shape=(jax.ShapeDtypeStruct((steps, LANES), BF16),) * count,
        in_specs=[vmem()] * 3,
        out_specs=(vmem(),) * count,
        cost_estimate=cost(2 * count * steps * rows * LANES, 2 * count * rows * LANES),
        compiler_params=pltpu.CompilerParams(vmem_limit_bytes=MID),
        name="more_partial",
    )(scat, phi, got)


def coef_kernel(gains_ref, zr_ref, zi_ref, drive_ref, shapes_ref,
                cr_ref, ci_ref, qr_ref, qi_ref, pre_ref, whole_ref, staged_ref, sems):
    tall = staged_ref.shape[0] // 8
    copies = []
    for q in range(8):
        part = pl.ds(q * tall, tall)
        copies.append(pltpu.make_async_copy(shapes_ref.at[part], staged_ref.at[part], sems.at[q]))
    for copy in copies:
        copy.start()
    steps = gains_ref.shape[1]
    inner = steps // 8
    row = lax.broadcasted_iota(jnp.int32, (steps, steps), 0)
    wanted = lax.rem(row, 8) * inner + lax.div(row, 8)
    hit = lax.broadcasted_iota(jnp.int32, (steps, steps), 1) == wanted
    left = gains_ref[...]
    gain_all = jnp.zeros((steps, LANES), F32)
    ones = jnp.ones((steps, LANES), BF16)
    for _ in range(3):
        term = left.astype(BF16)
        left = left - term.astype(F32)
        chosen = jnp.where(hit, term.astype(F32), 0.0).astype(BF16)
        gain_all = gain_all + jnp.dot(chosen, ones, preferred_element_type=F32)
    zr = zr_ref[...]
    zi = zi_ref[...]
    qr = jnp.ones((8, LANES), F32)
    qi = jnp.zeros((8, LANES), F32)
    for j in range(inner):
        gain = gain_all[8 * j : 8 * j + 8, :]
        cr = gain * zr
        ci = gain * zi
        cr_ref[j] = cr
        ci_ref[j] = ci
        qr, qi = qr * cr - qi * ci, qr * ci + qi * cr
        qr_ref[j] = qr
        qi_ref[j] = qi
    pr = jnp.ones((1, LANES), F32)
    pi = jnp.zeros((1, LANES), F32)
    for b in range(8):
        pre_ref[0, b : b + 1, :] = pr
        pre_ref[1, b : b + 1, :] = pi
        br = qr[b : b + 1, :]
        bi = qi[b : b + 1, :]
        pr, pi = pr * br - pi * bi, pr * bi + pi * br
    whole_ref[0:1, :] = pr
    whole_ref[1:2, :] = pi
    whole_ref[2:3, :] = drive_ref[...]
    whole_ref[3:8, :] = jnp.zeros((5, LANES), F32)
    for copy in copies:
        copy.wait()


def coefficients(gains, zr, zi, drive, shapes):
    inner = gains.shape[1] // 8
    full = jax.ShapeDtypeStruct((inner, 8, LANES), F32)
    return pl.pallas_call(
        coef_kernel,
        out_shape=(
            full,
            full,
            full,
            full,
            jax.ShapeDtypeStruct((2, 8, LANES), F32),
            jax.ShapeDtypeStruct((8, LANES), F32),
            pltpu.VMEM(shapes.shape, shapes.dtype),
        ),
        in_specs=[vmem()] * 4 + [hbm()],
        out_specs=(vmem(),) * 7,
        scratch_shapes=[pltpu.SemaphoreType.DMA((8,))],
        cost_estimate=cost(inner * 64 * LANES, 2 * shapes.size),
        compiler_params=pltpu.CompilerParams(vmem_limit_bytes=MID),
        name="coefficients",
    )(gains, zr, zi, drive, in_hbm(shapes))


def local_kernel(*refs):
    parts = refs[:-9]
    cr_ref, ci_ref, qr_ref, qi_ref, whole_ref, w_ref, enter_ref, send_ref, push_ref = refs[-9:]
    steps = parts[0].shape[0]
    inner = steps // 8
    drive = whole_ref[2:3, :]
    tile = 64
    for s in range(0, steps, tile):
        total = parts[0][s : s + tile, :].astype(F32)
        for part in parts[1:]:
            total += part[s : s + tile, :].astype(F32)
        total = total * drive
        for h in range(2):
            push_ref[h, s : s + tile, :] = total[:, h * HALF : (h + 1) * HALF]
    wr = jnp.zeros((8, LANES), F32)
    wi = jnp.zeros((8, LANES), F32)
    for j in range(inner):
        push = jnp.concatenate(
            [push_ref[h, pl.ds(j, 8, stride=inner), :] for h in range(2)], axis=1
        )
        cr = cr_ref[j]
        ci = ci_ref[j]
        wr, wi = cr * wr - ci * wi + push, cr * wi + ci * wr
        w_ref[j] = wr
    qr = qr_ref[inner - 1]
    qi = qi_ref[inner - 1]
    sr = jnp.zeros((1, LANES), F32)
    si = jnp.zeros((1, LANES), F32)
    for b in range(8):
        enter_ref[0, b : b + 1, :] = sr
        enter_ref[1, b : b + 1, :] = si
        br = qr[b : b + 1, :]
        bi = qi[b : b + 1, :]
        sr, si = (
            br * sr - bi * si + wr[b : b + 1, :],
            br * si + bi * sr + wi[b : b + 1, :],
        )
    row = lax.broadcasted_iota(jnp.int32, (8, LANES), 0)
    tile = jnp.where(row == 0, sr, jnp.where(row == 1, si, 0.0))
    tile = jnp.where(row == 2, whole_ref[0:1, :], jnp.where(row == 3, whole_ref[1:2, :], tile))
    for k in range(send_ref.shape[0]):
        send_ref[k] = tile


def local_recurrence(parts, cr, ci, qr, qi, whole, groups):
    count, steps = len(parts), parts[0].shape[0]
    inner = steps // 8
    return pl.pallas_call(
        local_kernel,
        out_shape=(
            jax.ShapeDtypeStruct((inner, 8, LANES), F32),
            jax.ShapeDtypeStruct((2, 8, LANES), F32),
            jax.ShapeDtypeStruct((groups, 8, LANES), F32),
        ),
        in_specs=[vmem()] * (count + 5),
        out_specs=(vmem(),) * 3,
        scratch_shapes=[pltpu.VMEM((2, steps, HALF), F32)],
        compiler_params=pltpu.CompilerParams(vmem_limit_bytes=MID),
        cost_estimate=cost(steps * LANES * 16, steps * LANES * (2 * count + 12)),
        name="local_recurrence",
    )(*parts, cr, ci, qr, qi, whole)


def history_kernel(got_ref, enter_ref, pre_ref, w_ref, qr_ref, qi_ref, history_ref, out_ref, hist_ref):
    inner = w_ref.shape[0]
    mine = lax.axis_index(TM)
    sr = jnp.zeros((1, LANES), F32)
    si = jnp.zeros((1, LANES), F32)
    for k in range(got_ref.shape[0] - 1):
        tile = got_ref[k]
        br, bi, ar, ai = (tile[r : r + 1, :] for r in range(4))
        nr = ar * sr - ai * si + br
        ni = ar * si + ai * sr + bi
        take = mine > k
        sr = jnp.where(take, nr, sr)
        si = jnp.where(take, ni, si)
    er = enter_ref[0] + pre_ref[0] * sr - pre_ref[1] * si
    ei = enter_ref[1] + pre_ref[0] * si + pre_ref[1] * sr
    for j in range(inner):
        value = w_ref[j] + qr_ref[j] * er - qi_ref[j] * ei
        for h in range(2):
            hist_ref[h, pl.ds(j, 8, stride=inner), :] = value[:, h * HALF : (h + 1) * HALF]
    natural = jnp.concatenate([hist_ref[h] for h in range(2)], axis=1)
    history_ref[...] = natural
    rounded = natural.astype(BF16)
    out_ref[...] = rounded


def make_history(got, enter, pre, w, qr, qi):
    inner = w.shape[0]
    steps = inner * 8
    return pl.pallas_call(
        history_kernel,
        out_shape=(
            jax.ShapeDtypeStruct((steps, LANES), F32),
            jax.ShapeDtypeStruct((steps, LANES), BF16),
        ),
        in_specs=[vmem()] * 6,
        out_specs=(vmem(), vmem()),
        scratch_shapes=[pltpu.VMEM((2, steps, HALF), F32)],
        compiler_params=pltpu.CompilerParams(vmem_limit_bytes=MID),
        cost_estimate=cost(steps * LANES * 4, steps * LANES * 18),
        name="make_history",
    )(got, enter, pre, w, qr, qi)


WIDE = 512


def field_tiles(whose, held, before, shapes_ref, store):
    places = [block_of(step, -1, other) for step, other in whose]
    for n in range(0, shapes_ref.shape[1], WIDE):
        across = slice(n, n + WIDE)
        total = before[0][:, across] if before else None
        for place, part in zip(places, held):
            product = jnp.dot(
                part[...], shapes_ref[pl.ds(place, LANES), across], preferred_element_type=F32
            )
            total = product if total is None else total + product
        store(n, total)


def first_kernel(whose, shapes_ref, natural_ref, *refs):
    held, (out_ref, history_ref) = refs[:-2], refs[-2:]

    def store(n, total):
        out_ref[:, n : n + WIDE] = total
        first = n // WIDE * HALF
        if first < natural_ref.shape[0]:
            part = slice(first, first + HALF)
            for h in range(2):
                lanes = slice(h * HALF, (h + 1) * HALF)
                history_ref[lanes, part] = natural_ref[part, lanes].T

    field_tiles(whose, held, [], shapes_ref, store)


def first_field(whose, held, staged, natural):
    steps, lanes = natural.shape
    points = staged.shape[1]
    return pl.pallas_call(
        lambda *refs: first_kernel(whose, *refs),
        out_shape=(
            jax.ShapeDtypeStruct((steps, points), F32),
            jax.ShapeDtypeStruct((lanes, steps), F32),
        ),
        in_specs=[vmem()] * (2 + len(held)),
        out_specs=(vmem(),) * 2,
        compiler_params=pltpu.CompilerParams(vmem_limit_bytes=MID),
        cost_estimate=cost(FLOPS * len(held), FLOPS),
        name="first_field",
    )(staged, natural, *held)


def next_kernel(whose, shapes_ref, before_ref, *refs):
    def store(n, total):
        refs[-1][:, n : n + WIDE] = total

    field_tiles(whose, refs[:-1], [before_ref], shapes_ref, store)


def next_field(whose, held, staged, before):
    return pl.pallas_call(
        lambda *refs: next_kernel(whose, *refs),
        out_shape=jax.ShapeDtypeStruct(before.shape, F32),
        in_specs=[vmem()] * (2 + len(held)),
        out_specs=vmem(),
        compiler_params=pltpu.CompilerParams(vmem_limit_bytes=MID),
        cost_estimate=cost(FLOPS * len(whose), FLOPS),
        name="next_field",
    )(staged, before, *held)


def last_kernel(whose, shapes_ref, before_ref, *refs):
    held, (out_hbm, out_ref, sems) = refs[:-3], refs[-3:]
    copies = []

    def store(n, total):
        out_ref[:, n : n + WIDE] = total.astype(BF16)
        across = pl.ds(n, WIDE)
        copy = pltpu.make_async_copy(
            out_ref.at[:, across], out_hbm.at[:, across], sems.at[n // WIDE]
        )
        copy.start()
        copies.append(copy)

    field_tiles(whose, held, [before_ref], shapes_ref, store)
    for copy in copies:
        copy.wait()


def last_field(whose, held, staged, before):
    steps, points = before.shape
    return pl.pallas_call(
        lambda *refs: last_kernel(whose, *refs),
        out_shape=jax.ShapeDtypeStruct((steps, points), BF16),
        in_specs=[vmem()] * (2 + len(held)),
        out_specs=hbm(),
        scratch_shapes=[
            pltpu.VMEM((steps, points), BF16),
            pltpu.SemaphoreType.DMA((points // WIDE,)),
        ],
        compiler_params=pltpu.CompilerParams(vmem_limit_bytes=MID),
        cost_estimate=cost(FLOPS * len(whose), FLOPS),
        name="last_field",
    )(staged, before, *held)


def step_pairs(dx, dy):
    nx, ny = 4, 2
    return [
        (x * ny + y, (x + dx) % nx * ny + (y + dy) % ny) for x in range(nx) for y in range(ny)
    ]


def body(loads, phi, load_index, damping, frequency, gains, shapes):
    steps = loads.shape[0]
    inner = steps // 8
    groups = lax.axis_size(TM)
    pair = [(0, 1), (1, 0)]
    scat, sent, held_phi = open_partial(load_index.reshape(1, -1), loads, phi)
    first = lax.ppermute(sent, "core", pair)
    sent = rest_partial(scat, held_phi)
    summed = list(more_partial(scat, held_phi, STEPS[:EARLY], first))
    sent, *summed = lax.optimization_barrier((sent, *summed))
    last = lax.ppermute(sent, "core", pair)
    summed += more_partial(scat, held_phi, STEPS[EARLY:], last)
    parts = []
    for step, part in zip(STEPS, summed):
        parts.append(part if step == (0, 0) else lax.ppermute(part, XY, step_pairs(*step)))

    radius = jnp.exp(-damping)
    zr = (radius * jnp.cos(frequency)).reshape(1, -1)
    zi = (radius * jnp.sin(frequency)).reshape(1, -1)
    drive = jnp.sqrt(-jnp.expm1(-2.0 * damping)).reshape(1, -1)
    late, parts[7] = lax.optimization_barrier((shapes, parts[7]))
    *coef, staged = coefficients(gains.reshape(1, -1), zr, zi, drive, late)
    cr, ci, qr, qi, pre, whole = coef
    w, enter, payload = local_recurrence(parts, cr, ci, qr, qi, whole, groups)
    states = lax.all_to_all(payload, TM, 0, 0)
    natural, mine = make_history(states, enter, pre, w, qr, qi)
    near = [lax.ppermute(mine, XY, step_pairs(*step)) for step in SPREAD]
    near.append(mine)
    whose = [*SPREAD, (0, 0)]

    def pick(chosen):
        return [(whose[q], False) for q in chosen], [near[q] for q in chosen]

    sent = list(near)
    field, history = first_field(*pick((7, 3, 1)), staged, natural)
    field, sent[0] = lax.optimization_barrier((field, sent[0]))
    field = next_field(*pick((0, 2, 4)), staged, field)
    field, sent[5] = lax.optimization_barrier((field, sent[5]))
    far = [lax.ppermute(part, "core", pair) for part in sent]
    field = next_field(*pick((5, 6)), staged, field)
    field = last_field([(step, True) for step in whose], far, staged, field)
    return field, history


def solution(mesh):
    grid = Mesh(mesh.devices.reshape(4, 2, 4, 2, 2), ("z", "yh", "x", "yl", "core"))
    placed = (
        P(TM, DOF),
        P(DOF, None),
        P(DOF),
        P(DOF),
        P(DOF),
        P(TM),
        P(None, DOF),
    )
    return jax.shard_map(
        body,
        mesh=grid,
        in_specs=placed,
        out_specs=(P(TM, DOF), P(DOF, TM)),
        check_vma=False,
    )
```

```python
import jax
import jax.numpy as jnp
from jax import lax
from jax.experimental import pallas as pl
from jax.experimental.pallas import tpu as pltpu
from jax.sharding import Mesh, PartitionSpec as P

TM = ("z", "yh")
XY = ("x", "yl")
DOF = ("x", "yl", "core")
F32 = jnp.float32
BF16 = jnp.bfloat16
LANES = 256
HALF = 128
MID = 12 * 1024 * 1024
DEEP = 256
EARLY = 2
FLOPS = 500 * 1000 * 1000
STEPS = ((2, 1), (3, 1), (1, 0), (2, 0), (0, 1), (3, 0), (1, 1), (0, 0))
SPREAD = ((2, 0), (2, 1), (1, 0), (0, 1), (3, 1), (1, 1), (3, 0))


def vmem():
    return pl.BlockSpec(memory_space=pltpu.VMEM)


def cost(flops, moved):
    return pl.CostEstimate(flops=int(flops), bytes_accessed=int(moved), transcendentals=0)


def smem():
    return pl.BlockSpec(memory_space=pltpu.SMEM)


def hbm():
    return pl.BlockSpec(memory_space=pltpu.HBM)


def in_hbm(value):
    return pltpu.with_memory_space_constraint(value, pltpu.HBM)


def block_of(step, sign, other):
    dx, dy = step
    x = lax.rem(lax.axis_index("x") + (4 + sign * dx) % 4, 4)
    y = lax.rem(lax.axis_index("yl") + dy, 2)
    core = lax.axis_index("core")
    core = 1 - core if other else core
    return pl.multiple_of((2 * (2 * x + y) + core) * LANES, LANES)


def products(scat_ref, phi_ref, steps, other, wait=None):
    places = [block_of(step, 1, other) for step in steps]
    total = None
    for k in range(0, phi_ref.shape[0], DEEP):
        if wait is not None:
            wait(k // DEEP)
        rows = slice(k, k + DEEP)
        block = jnp.concatenate([phi_ref[rows, pl.ds(place, LANES)] for place in places], axis=1)
        part = jnp.dot(scat_ref[:, rows], block, preferred_element_type=F32)
        total = part if total is None else total + part
    return [total[:, q * LANES : (q + 1) * LANES] for q in range(len(steps))]


def open_kernel(index_hbm, loads_hbm, phi_hbm, scat_ref, sent_ref, phi_ref,
                index_ref, loads_ref, sems, load_sems):
    index_copy = pltpu.make_async_copy(index_hbm, index_ref, load_sems.at[0])
    loads_copy = pltpu.make_async_copy(loads_hbm, loads_ref, load_sems.at[1])
    copies = []
    for q in range(phi_ref.shape[0] // DEEP):
        part = pl.ds(q * DEEP, DEEP)
        copies.append(pltpu.make_async_copy(phi_hbm.at[part], phi_ref.at[part], sems.at[q]))
    for copy in [index_copy, loads_copy] + copies:
        copy.start()
    rows = scat_ref.shape[1]
    channels = index_ref.shape[1]
    place = lax.broadcasted_iota(jnp.int32, (channels, rows), 1).astype(F32)
    index_copy.wait()
    local = (index_ref[...] - lax.axis_index(DOF) * rows).astype(F32)
    column = jnp.broadcast_to(local, (8, channels)).T[:, 0:1]
    onehot = jnp.where(place == column, 1.0, 0.0).astype(BF16)
    loads_copy.wait()
    summed = jnp.dot(loads_ref[...], onehot, preferred_element_type=F32)
    scat_ref[...] = summed.astype(BF16)
    mine = products(scat_ref, phi_ref, STEPS[:EARLY], True, lambda k: copies[k].wait())
    for q, value in enumerate(mine):
        sent_ref[q] = value.astype(BF16)


def open_partial(index_row, loads, phi):
    steps, channels = loads.shape
    rows = phi.shape[0]
    return pl.pallas_call(
        open_kernel,
        out_shape=(
            pltpu.VMEM((steps, rows), BF16),
            jax.ShapeDtypeStruct((EARLY, steps, LANES), BF16),
            pltpu.VMEM(phi.shape, BF16),
        ),
        in_specs=[hbm(), hbm(), hbm()],
        out_specs=(vmem(),) * 3,
        scratch_shapes=[
            pltpu.VMEM((1, channels), jnp.int32),
            pltpu.VMEM((steps, channels), BF16),
            pltpu.SemaphoreType.DMA((rows // DEEP,)),
            pltpu.SemaphoreType.DMA((2,)),
        ],
        cost_estimate=cost(2 * steps * rows * (channels + EARLY * LANES), 32 * rows * LANES),
        compiler_params=pltpu.CompilerParams(vmem_limit_bytes=MID),
        name="open_partial",
    )(in_hbm(index_row), in_hbm(loads), in_hbm(phi))


def rest_kernel(scat_ref, phi_ref, sent_ref):
    for q, value in enumerate(products(scat_ref, phi_ref, STEPS[EARLY:], True)):
        sent_ref[q] = value.astype(BF16)


def rest_partial(scat, phi):
    steps, rows = scat.shape
    return pl.pallas_call(
        rest_kernel,
        out_shape=jax.ShapeDtypeStruct((8 - EARLY, steps, LANES), BF16),
        in_specs=[vmem(), vmem()],
        out_specs=vmem(),
        cost_estimate=cost(8 * steps * rows * LANES, 8 * rows * LANES),
        compiler_params=pltpu.CompilerParams(vmem_limit_bytes=MID),
        name="rest_partial",
    )(scat, phi)


def more_kernel(chosen, scat_ref, phi_ref, got_ref, *outs):
    for q, value in enumerate(products(scat_ref, phi_ref, chosen, False)):
        outs[q][...] = (value + got_ref[q].astype(F32)).astype(BF16)


def more_partial(scat, phi, chosen, got):
    steps, rows = scat.shape
    count = len(chosen)
    return pl.pallas_call(
        lambda *refs: more_kernel(chosen, *refs),
        out_shape=(jax.ShapeDtypeStruct((steps, LANES), BF16),) * count,
        in_specs=[vmem()] * 3,
        out_specs=(vmem(),) * count,
        cost_estimate=cost(2 * count * steps * rows * LANES, 2 * count * rows * LANES),
        compiler_params=pltpu.CompilerParams(vmem_limit_bytes=MID),
        name="more_partial",
    )(scat, phi, got)


def coef_kernel(gains_ref, zr_ref, zi_ref, drive_ref, shapes_ref,
                cr_ref, ci_ref, qr_ref, qi_ref, pre_ref, whole_ref, staged_ref, sems):
    tall = staged_ref.shape[0] // 8
    copies = []
    for q in range(8):
        part = pl.ds(q * tall, tall)
        copies.append(pltpu.make_async_copy(shapes_ref.at[part], staged_ref.at[part], sems.at[q]))
    for copy in copies:
        copy.start()
    steps = gains_ref.shape[1]
    inner = steps // 8
    row = lax.broadcasted_iota(jnp.int32, (steps, steps), 0)
    wanted = lax.rem(row, 8) * inner + lax.div(row, 8)
    hit = lax.broadcasted_iota(jnp.int32, (steps, steps), 1) == wanted
    left = gains_ref[...]
    gain_all = jnp.zeros((steps, LANES), F32)
    ones = jnp.ones((steps, LANES), BF16)
    for _ in range(3):
        term = left.astype(BF16)
        left = left - term.astype(F32)
        chosen = jnp.where(hit, term.astype(F32), 0.0).astype(BF16)
        gain_all = gain_all + jnp.dot(chosen, ones, preferred_element_type=F32)
    zr = zr_ref[...]
    zi = zi_ref[...]
    qr = jnp.ones((8, LANES), F32)
    qi = jnp.zeros((8, LANES), F32)
    for j in range(inner):
        gain = gain_all[8 * j : 8 * j + 8, :]
        cr = gain * zr
        ci = gain * zi
        cr_ref[j] = cr
        ci_ref[j] = ci
        qr, qi = qr * cr - qi * ci, qr * ci + qi * cr
        qr_ref[j] = qr
        qi_ref[j] = qi
    pr = jnp.ones((1, LANES), F32)
    pi = jnp.zeros((1, LANES), F32)
    for b in range(8):
        pre_ref[0, b : b + 1, :] = pr
        pre_ref[1, b : b + 1, :] = pi
        br = qr[b : b + 1, :]
        bi = qi[b : b + 1, :]
        pr, pi = pr * br - pi * bi, pr * bi + pi * br
    whole_ref[0:1, :] = pr
    whole_ref[1:2, :] = pi
    whole_ref[2:3, :] = drive_ref[...]
    whole_ref[3:8, :] = jnp.zeros((5, LANES), F32)
    for copy in copies:
        copy.wait()


def coefficients(gains, zr, zi, drive, shapes):
    inner = gains.shape[1] // 8
    full = jax.ShapeDtypeStruct((inner, 8, LANES), F32)
    return pl.pallas_call(
        coef_kernel,
        out_shape=(
            full,
            full,
            full,
            full,
            jax.ShapeDtypeStruct((2, 8, LANES), F32),
            jax.ShapeDtypeStruct((8, LANES), F32),
            pltpu.VMEM(shapes.shape, shapes.dtype),
        ),
        in_specs=[vmem()] * 4 + [hbm()],
        out_specs=(vmem(),) * 7,
        scratch_shapes=[pltpu.SemaphoreType.DMA((8,))],
        cost_estimate=cost(inner * 64 * LANES, 2 * shapes.size),
        compiler_params=pltpu.CompilerParams(vmem_limit_bytes=MID),
        name="coefficients",
    )(gains, zr, zi, drive, in_hbm(shapes))


def local_kernel(*refs):
    parts = refs[:-9]
    cr_ref, ci_ref, qr_ref, qi_ref, whole_ref, w_ref, enter_ref, send_ref, push_ref = refs[-9:]
    steps = parts[0].shape[0]
    inner = steps // 8
    drive = whole_ref[2:3, :]
    tile = 64
    for s in range(0, steps, tile):
        total = parts[0][s : s + tile, :].astype(F32)
        for part in parts[1:]:
            total += part[s : s + tile, :].astype(F32)
        total = total * drive
        for h in range(2):
            push_ref[h, s : s + tile, :] = total[:, h * HALF : (h + 1) * HALF]
    wr = jnp.zeros((8, LANES), F32)
    wi = jnp.zeros((8, LANES), F32)
    for j in range(inner):
        push = jnp.concatenate(
            [push_ref[h, pl.ds(j, 8, stride=inner), :] for h in range(2)], axis=1
        )
        cr = cr_ref[j]
        ci = ci_ref[j]
        wr, wi = cr * wr - ci * wi + push, cr * wi + ci * wr
        w_ref[j] = wr
    qr = qr_ref[inner - 1]
    qi = qi_ref[inner - 1]
    sr = jnp.zeros((1, LANES), F32)
    si = jnp.zeros((1, LANES), F32)
    for b in range(8):
        enter_ref[0, b : b + 1, :] = sr
        enter_ref[1, b : b + 1, :] = si
        br = qr[b : b + 1, :]
        bi = qi[b : b + 1, :]
        sr, si = (
            br * sr - bi * si + wr[b : b + 1, :],
            br * si + bi * sr + wi[b : b + 1, :],
        )
    row = lax.broadcasted_iota(jnp.int32, (8, LANES), 0)
    tile = jnp.where(row == 0, sr, jnp.where(row == 1, si, 0.0))
    tile = jnp.where(row == 2, whole_ref[0:1, :], jnp.where(row == 3, whole_ref[1:2, :], tile))
    for k in range(send_ref.shape[0]):
        send_ref[k] = tile


def local_recurrence(parts, cr, ci, qr, qi, whole, groups):
    count, steps = len(parts), parts[0].shape[0]
    inner = steps // 8
    return pl.pallas_call(
        local_kernel,
        out_shape=(
            jax.ShapeDtypeStruct((inner, 8, LANES), F32),
            jax.ShapeDtypeStruct((2, 8, LANES), F32),
            jax.ShapeDtypeStruct((groups, 8, LANES), F32),
        ),
        in_specs=[vmem()] * (count + 5),
        out_specs=(vmem(),) * 3,
        scratch_shapes=[pltpu.VMEM((2, steps, HALF), F32)],
        compiler_params=pltpu.CompilerParams(vmem_limit_bytes=MID),
        cost_estimate=cost(steps * LANES * 16, steps * LANES * (2 * count + 12)),
        name="local_recurrence",
    )(*parts, cr, ci, qr, qi, whole)


def history_kernel(got_ref, enter_ref, pre_ref, w_ref, qr_ref, qi_ref, history_ref, out_ref, hist_ref):
    inner = w_ref.shape[0]
    mine = lax.axis_index(TM)
    sr = jnp.zeros((1, LANES), F32)
    si = jnp.zeros((1, LANES), F32)
    for k in range(got_ref.shape[0] - 1):
        tile = got_ref[k]
        br, bi, ar, ai = (tile[r : r + 1, :] for r in range(4))
        nr = ar * sr - ai * si + br
        ni = ar * si + ai * sr + bi
        take = mine > k
        sr = jnp.where(take, nr, sr)
        si = jnp.where(take, ni, si)
    er = enter_ref[0] + pre_ref[0] * sr - pre_ref[1] * si
    ei = enter_ref[1] + pre_ref[0] * si + pre_ref[1] * sr
    for j in range(inner):
        value = w_ref[j] + qr_ref[j] * er - qi_ref[j] * ei
        for h in range(2):
            hist_ref[h, pl.ds(j, 8, stride=inner), :] = value[:, h * HALF : (h + 1) * HALF]
    natural = jnp.concatenate([hist_ref[h] for h in range(2)], axis=1)
    history_ref[...] = natural
    rounded = natural.astype(BF16)
    out_ref[...] = rounded


def make_history(got, enter, pre, w, qr, qi):
    inner = w.shape[0]
    steps = inner * 8
    return pl.pallas_call(
        history_kernel,
        out_shape=(
            jax.ShapeDtypeStruct((steps, LANES), F32),
            jax.ShapeDtypeStruct((steps, LANES), BF16),
        ),
        in_specs=[vmem()] * 6,
        out_specs=(vmem(), vmem()),
        scratch_shapes=[pltpu.VMEM((2, steps, HALF), F32)],
        compiler_params=pltpu.CompilerParams(vmem_limit_bytes=MID),
        cost_estimate=cost(steps * LANES * 4, steps * LANES * 18),
        name="make_history",
    )(got, enter, pre, w, qr, qi)


WIDE = 512


def field_tiles(whose, held, before, shapes_ref, store):
    places = [block_of(step, -1, other) for step, other in whose]
    for n in range(0, shapes_ref.shape[1], WIDE):
        across = slice(n, n + WIDE)
        total = before[0][:, across] if before else None
        for place, part in zip(places, held):
            product = jnp.dot(
                part[...], shapes_ref[pl.ds(place, LANES), across], preferred_element_type=F32
            )
            total = product if total is None else total + product
        store(n, total)


def first_kernel(whose, shapes_ref, natural_ref, *refs):
    held, (out_ref, history_ref) = refs[:-2], refs[-2:]

    def store(n, total):
        out_ref[:, n : n + WIDE] = total
        first = n // WIDE * HALF
        if first < natural_ref.shape[0]:
            part = slice(first, first + HALF)
            for h in range(2):
                lanes = slice(h * HALF, (h + 1) * HALF)
                history_ref[lanes, part] = natural_ref[part, lanes].T

    field_tiles(whose, held, [], shapes_ref, store)


def first_field(whose, held, staged, natural):
    steps, lanes = natural.shape
    points = staged.shape[1]
    return pl.pallas_call(
        lambda *refs: first_kernel(whose, *refs),
        out_shape=(
            jax.ShapeDtypeStruct((steps, points), F32),
            jax.ShapeDtypeStruct((lanes, steps), F32),
        ),
        in_specs=[vmem()] * (2 + len(held)),
        out_specs=(vmem(),) * 2,
        compiler_params=pltpu.CompilerParams(vmem_limit_bytes=MID),
        cost_estimate=cost(FLOPS * len(held), FLOPS),
        name="first_field",
    )(staged, natural, *held)


def next_kernel(whose, shapes_ref, before_ref, *refs):
    def store(n, total):
        refs[-1][:, n : n + WIDE] = total

    field_tiles(whose, refs[:-1], [before_ref], shapes_ref, store)


def next_field(whose, held, staged, before):
    return pl.pallas_call(
        lambda *refs: next_kernel(whose, *refs),
        out_shape=jax.ShapeDtypeStruct(before.shape, F32),
        in_specs=[vmem()] * (2 + len(held)),
        out_specs=vmem(),
        compiler_params=pltpu.CompilerParams(vmem_limit_bytes=MID),
        cost_estimate=cost(FLOPS * len(whose), FLOPS),
        name="next_field",
    )(staged, before, *held)


def last_kernel(whose, shapes_ref, before_ref, *refs):
    held, (out_hbm, out_ref, sems) = refs[:-3], refs[-3:]
    copies = []

    def store(n, total):
        out_ref[:, n : n + WIDE] = total.astype(BF16)
        across = pl.ds(n, WIDE)
        copy = pltpu.make_async_copy(
            out_ref.at[:, across], out_hbm.at[:, across], sems.at[n // WIDE]
        )
        copy.start()
        copies.append(copy)

    field_tiles(whose, held, [before_ref], shapes_ref, store)
    for copy in copies:
        copy.wait()


def last_field(whose, held, staged, before):
    steps, points = before.shape
    return pl.pallas_call(
        lambda *refs: last_kernel(whose, *refs),
        out_shape=jax.ShapeDtypeStruct((steps, points), BF16),
        in_specs=[vmem()] * (2 + len(held)),
        out_specs=hbm(),
        scratch_shapes=[
            pltpu.VMEM((steps, points), BF16),
            pltpu.SemaphoreType.DMA((points // WIDE,)),
        ],
        compiler_params=pltpu.CompilerParams(vmem_limit_bytes=MID),
        cost_estimate=cost(FLOPS * len(whose), FLOPS),
        name="last_field",
    )(staged, before, *held)


def step_pairs(dx, dy):
    nx, ny = 4, 2
    return [
        (x * ny + y, (x + dx) % nx * ny + (y + dy) % ny) for x in range(nx) for y in range(ny)
    ]


def body(loads, phi, load_index, damping, frequency, gains, shapes):
    steps = loads.shape[0]
    inner = steps // 8
    groups = lax.axis_size(TM)
    pair = [(0, 1), (1, 0)]
    scat, sent, held_phi = open_partial(load_index.reshape(1, -1), loads, phi)
    first = lax.ppermute(sent, "core", pair)
    sent = rest_partial(scat, held_phi)
    summed = list(more_partial(scat, held_phi, STEPS[:EARLY], first))
    sent, *summed = lax.optimization_barrier((sent, *summed))
    last = lax.ppermute(sent, "core", pair)
    summed += more_partial(scat, held_phi, STEPS[EARLY:], last)
    parts = []
    for step, part in zip(STEPS, summed):
        parts.append(part if step == (0, 0) else lax.ppermute(part, XY, step_pairs(*step)))

    radius = jnp.exp(-damping)
    zr = (radius * jnp.cos(frequency)).reshape(1, -1)
    zi = (radius * jnp.sin(frequency)).reshape(1, -1)
    drive = jnp.sqrt(-jnp.expm1(-2.0 * damping)).reshape(1, -1)
    late, parts[7] = lax.optimization_barrier((shapes, parts[7]))
    *coef, staged = coefficients(gains.reshape(1, -1), zr, zi, drive, late)
    cr, ci, qr, qi, pre, whole = coef
    w, enter, payload = local_recurrence(parts, cr, ci, qr, qi, whole, groups)
    states = lax.all_to_all(payload, TM, 0, 0)
    natural, mine = make_history(states, enter, pre, w, qr, qi)
    near = [lax.ppermute(mine, XY, step_pairs(*step)) for step in SPREAD]
    near.append(mine)
    whose = [*SPREAD, (0, 0)]

    def pick(chosen):
        return [(whose[q], False) for q in chosen], [near[q] for q in chosen]

    sent = list(near)
    field, history = first_field(*pick((7, 3, 1)), staged, natural)
    field, sent[0] = lax.optimization_barrier((field, sent[0]))
    field = next_field(*pick((0, 2, 4)), staged, field)
    field, sent[5] = lax.optimization_barrier((field, sent[5]))
    far = [lax.ppermute(part, "core", pair) for part in sent]
    field = next_field(*pick((5, 6)), staged, field)
    field = last_field([(step, True) for step in whose], far, staged, field)
    return field, history


def solution(mesh):
    grid = Mesh(mesh.devices.reshape(4, 2, 4, 2, 2), ("z", "yh", "x", "yl", "core"))
    placed = (
        P(TM, DOF),
        P(DOF, None),
        P(DOF),
        P(DOF),
        P(DOF),
        P(TM),
        P(None, DOF),
    )
    return jax.shard_map(
        body,
        mesh=grid,
        in_specs=placed,
        out_specs=(P(TM, DOF), P(DOF, TM)),
        check_vma=False,
    )
```
